768 devices in a mesh: ctx: 192 (over y, z, core), head: 4 (over x).
Axes of the slice: x: 4, y: 8, z: 12, core: 2. Of those that a mesh axis runs over, the one named last changes fastest.
Arguments:
- queries: bfloat16 [49152, 256], P('ctx', 'head'), may hold values from -6 to 6
- keys: bfloat16 [49152, 256], P('ctx', 'head'), may hold values from -6 to 6
- values: bfloat16 [49152, 2048], P('ctx', 'head'), may hold values from -6 to 6
- conv_keys: float32 [3, 256], P(None, 'head'), may hold values from -3.5 to 3.5
- conv_values: float32 [3, 2048], P(None, 'head'), may hold values from -3.5 to 3.5
- out_weight: bfloat16 [2048, 2048], P('head'), may hold values from -0.125 to 0.125
- cotangent: bfloat16 [49152, 2048], P('ctx', 'head'), may hold values from -6 to 6
Outputs:
- mixed_out: bfloat16 [49152, 2048], P('ctx', 'head')
- value_grad: bfloat16 [49152, 2048], P('ctx', 'head')
The draws below stay inside these ranges and needn't reach their ends.
All inputs are finite; a program needn't handle non-finite values.
Results may differ from the reference program's by a relative error of at most 0.004.
The reference program's roundings to bfloat16 on the way count: a program that leaves them out, or rounds other values in their place, can miss the bound.
Values may be sent and summed in bfloat16 or wider, within the bound.
A program may use at most 32 MiB of HBM per device.

```python
import jax
import jax.numpy as jnp
from jax import lax

D = 2048
HEADS = 16
FEAT = 16
VDIM = 128
CONV = 3
TOK_DEV = 256
PHI = 273
TOKENS = 49152


def block_levels(stream_key, dims, cuts, least, high):
    gain, own = 1.0, jax.random.fold_in(stream_key, 6)
    for axis_at, blocks in cuts:
        draws = jnp.exp(jax.random.uniform(jax.random.fold_in(own, axis_at), (blocks,), jnp.float32, least / len(cuts), high / len(cuts)))
        gain = gain * jnp.repeat(draws, dims[axis_at] // blocks).reshape([-1 if axis == axis_at else 1 for axis in range(len(dims))])
    return gain


def bell_draw(own_key, dims, deviation, bound, cuts=(), kind=jnp.bfloat16):
    drawn = jax.random.normal(own_key, dims, jnp.float32) * deviation
    if len(cuts) > 0:
        drawn = block_levels(own_key, dims, cuts, -0.22, 0.18) * drawn
    return jnp.clip(drawn, min=-bound, max=bound).astype(kind)


def setup_inputs(seed: int = 0) -> dict:
    streams_of = jax.random.split(jax.random.key(seed), 8)
    queries = bell_draw(streams_of[0], (TOKENS, HEADS * FEAT), 1.0, 6.0, ((0, 192), (1, 4)))
    keys = bell_draw(streams_of[1], (TOKENS, HEADS * FEAT), 1.0, 6.0, ((0, 192), (1, 4)))
    values = bell_draw(streams_of[2], (TOKENS, HEADS * VDIM), 1.0, 6.0, ((0, 192), (1, 4)))
    conv_keys = bell_draw(streams_of[3], (CONV, HEADS * FEAT), CONV ** -0.5, 3.5, ((1, 4),), jnp.float32)
    conv_values = bell_draw(streams_of[4], (CONV, HEADS * VDIM), CONV ** -0.5, 3.5, ((1, 4),), jnp.float32)
    out_weight = bell_draw(streams_of[5], (HEADS * VDIM, D), (HEADS * VDIM) ** -0.5, 0.125, ((0, 4),))
    cotangent = bell_draw(streams_of[6], (TOKENS, D), 1.0, 6.0, ((0, 192), (1, 4)))
    return dict(queries=queries, keys=keys, values=values, conv_keys=conv_keys, conv_values=conv_values, out_weight=out_weight, cotangent=cotangent)


def features(inputs):
    scaled = inputs * FEAT ** -0.25
    square = scaled[..., :, None] * scaled[..., None, :]
    square = square.reshape(scaled.shape[:-1] + (FEAT * FEAT,)) * 0.5 ** 0.5
    constant = jnp.ones(scaled.shape[:-1] + (1,), jnp.float32)
    return jnp.concatenate([constant, scaled, square], -1).astype(jnp.bfloat16)


def convolve(token_block, before, weights):
    joined = jnp.concatenate([before, token_block], 0).astype(jnp.float32)
    block_rows = token_block.shape[0]
    running = weights[0] * joined[CONV - 1:CONV - 1 + block_rows]
    for offset in range(1, CONV):
        running = running + weights[offset] * joined[CONV - 1 - offset:CONV - 1 - offset + block_rows]
    return running


def lowered(array_in):
    return lax.optimization_barrier(array_in.astype(jnp.bfloat16)).astype(jnp.float32)


def reference(queries, keys, values, conv_keys, conv_values, out_weight, cotangent):
    highest = lax.Precision.HIGHEST
    key_conv = convolve(keys, jnp.zeros((CONV - 1, keys.shape[1]), jnp.bfloat16), conv_keys)
    value_conv = convolve(values, jnp.zeros((CONV - 1, values.shape[1]), jnp.bfloat16), conv_values).astype(jnp.bfloat16)
    blocks = TOKENS // TOK_DEV
    query_blocks = queries.reshape(blocks, TOK_DEV, HEADS, FEAT)
    key_blocks = key_conv.reshape(blocks, TOK_DEV, HEADS, FEAT)
    value_blocks = value_conv.reshape(blocks, TOK_DEV, HEADS, VDIM)
    causal = jnp.arange(TOK_DEV)[:, None] >= jnp.arange(TOK_DEV)[None, :]

    def block_scores(query_feat, key_feat):
        scores = jnp.einsum("thp,shp->hts", query_feat.astype(jnp.float32), key_feat.astype(jnp.float32), precision=highest)
        return jnp.where(causal[None], scores, 0.0)

    def forward_step(running, block_items):
        value_state, norm_sum = running
        query_raw, key_raw, value_block = block_items
        query_feat = features(query_raw.astype(jnp.float32))
        key_feat = features(key_raw)
        scores = block_scores(query_feat, key_feat)
        scores_low = lowered(scores)
        query_wide = query_feat.astype(jnp.float32)
        key_wide = key_feat.astype(jnp.float32)
        value_wide = value_block.astype(jnp.float32)
        numerator = jnp.einsum("hts,shv->thv", scores_low, value_wide, precision=highest)
        numerator = numerator + jnp.einsum("thp,hpv->thv", query_wide, lowered(value_state), precision=highest)
        denominator = jnp.sum(scores, 2).T + jnp.einsum("thp,hp->th", query_wide, norm_sum, precision=highest)
        attended = (numerator / denominator[..., None]).astype(jnp.bfloat16)
        value_state = value_state + jnp.einsum("shp,shv->hpv", key_wide, value_wide, precision=highest)
        norm_sum = norm_sum + jnp.sum(key_wide, 0)
        return (value_state, norm_sum), (attended, denominator)

    start_state = (jnp.zeros((HEADS, PHI, VDIM), jnp.float32), jnp.zeros((HEADS, PHI), jnp.float32))
    _, (attended, denominator) = lax.scan(forward_step, start_state, (query_blocks, key_blocks, value_blocks))
    attended = attended.reshape(TOKENS, HEADS * VDIM)
    mixed_out = jnp.dot(attended, out_weight, preferred_element_type=jnp.float32).astype(jnp.bfloat16)
    out_grad = jnp.dot(cotangent, out_weight.T, preferred_element_type=jnp.float32)
    scaled_grad = (out_grad.reshape(blocks, TOK_DEV, HEADS, VDIM) / denominator[..., None]).astype(jnp.bfloat16)

    def backward_step(later_state, block_items):
        query_raw, key_raw, grad_block = block_items
        query_feat = features(query_raw.astype(jnp.float32))
        key_feat = features(key_raw)
        scores_low = lowered(block_scores(query_feat, key_feat))
        grad_wide = grad_block.astype(jnp.float32)
        grad_here = jnp.einsum("hts,thv->shv", scores_low, grad_wide, precision=highest)
        grad_here = grad_here + jnp.einsum("shp,hpv->shv", key_feat.astype(jnp.float32), lowered(later_state), precision=highest)
        later_state = later_state + jnp.einsum("thp,thv->hpv", query_feat.astype(jnp.float32), grad_wide, precision=highest)
        return later_state, grad_here.astype(jnp.bfloat16)

    _, value_grad = lax.scan(backward_step, jnp.zeros((HEADS, PHI, VDIM), jnp.float32), (query_blocks, key_blocks, scaled_grad), reverse=True)
    return mixed_out, value_grad.reshape(TOKENS, HEADS * VDIM)
```

```python
import functools

import jax
import jax.numpy as jnp
from jax import lax
from jax.experimental import pallas as pl
from jax.experimental.pallas import tpu as pltpu
from jax.sharding import PartitionSpec as P

FEAT = 16
VDIM = 128
CONV = 3
NY, NZ, NX = 8, 12, 4
TOK = 256
ROWS = 160
GROUPS = ROWS // 16
NORM = GROUPS
HALO = 16
BF = jnp.bfloat16
F32 = jnp.float32


def mm(a, b):
    return jnp.dot(a, b, preferred_element_type=F32)


def mm_t(a, b):
    return lax.dot_general(a, b, (((1,), (1,)), ((), ())), preferred_element_type=F32)


def remote(src, dst, send, recv, ctx, head):
    return pltpu.make_async_remote_copy(
        src_ref=src,
        dst_ref=dst,
        send_sem=send,
        recv_sem=recv,
        device_id=(ctx, head),
        device_id_type=pl.DeviceIdType.MESH,
    )


def build_features(raw, row0, query, store):
    s = raw[pl.ds(row0, FEAT), :] * FEAT ** (-0.25)
    half = 0.5**0.5
    pair = 2.0 * half if query else half
    store[0:16, :] = s * s * half
    for d in range(1, 8):
        store[16 * d : 16 * d + 16, :] = s * pltpu.roll(s, FEAT - d, 0) * pair
    store[128:136, :] = s[0:8] * s[8:16] * pair
    row = lax.broadcasted_iota(jnp.int32, (8, s.shape[1]), 0)
    store[136:144, :] = jnp.where(row == 0, 1.0, 0.0)
    store[144:160, :] = s


def body(
    q_hbm, k_hbm, v_hbm, ck_ref, cv_ref, w_hbm, cot_hbm, mixed_ref, vgrad_ref,
    qb, kb, vb, w, cotg, raw, feat, q_pt, q_tp, k_pt, k_tp, vc, wl, wlt, dsum,
    state0, total, a1, n1, r1, rn, tsum, tnorm, ry, ryn, base, basen, qo, qn, pr, pn,
    og, ogs, grad, u1, a2, r2, t2, ry2, qo2, pr2, att, atts, vgs,
    rs1s, rs1r, rs2s, rs2r,
    loc, ex_s, ex_r, halo_s, halo_r, p1_s, p1_r, y_s, y_r, p3_s, p3_r,
    g1_s, g1_r, gy_s, gy_r, g3_s, g3_r, ag_s, ag_r, rs_s, rs_r, misc_s, misc_r,
):
    ctx = lax.axis_index("ctx")
    x = lax.axis_index("head")
    y = lax.div(ctx, 2 * NZ)
    chip = lax.div(ctx, 2)
    z = lax.rem(chip, NZ)
    c = lax.rem(ctx, 2)
    sib = chip * 2 + 1 - c
    chips = NY * NZ
    before = lax.rem(chip + chips - 1, chips)
    after = lax.rem(chip + 1, chips)
    right, left = lax.rem(x + 1, NX), lax.rem(x + NX - 1, NX)
    far = lax.rem(x + 2, NX)

    def at(y_, z_):
        return (y_ * NZ + z_) * 2 + c

    load_w = pltpu.make_async_copy(w_hbm, w, loc.at[0])
    load_w.start()
    mine = pl.ds(pl.multiple_of(HALO + TOK * c, 16), TOK)
    own_lanes = pl.ds(pl.multiple_of(256 * c, 256), 256)
    sib_lanes = pl.ds(pl.multiple_of(256 * (1 - c), 256), 256)
    load_k = pltpu.make_async_copy(k_hbm, kb.at[mine, :], loc.at[1])
    load_v = pltpu.make_async_copy(v_hbm.at[:, own_lanes], vb.at[mine, :], loc.at[2])
    load_q = pltpu.make_async_copy(q_hbm, qb.at[c], loc.at[3])
    load_c = pltpu.make_async_copy(cot_hbm, cotg.at[x], loc.at[4])
    for copy in (load_k, load_v, load_q, load_c):
        copy.start()

    barrier = pltpu.get_barrier_semaphore()

    def greet(ctx_, x_):
        pl.semaphore_signal(
            barrier, inc=1, device_id=(ctx_, x_), device_id_type=pl.DeviceIdType.MESH
        )

    greet(sib, x)
    greet(before * 2 + 1, x)
    greet(ctx, right)
    greet(ctx, left)
    for d in range(1, NZ):
        greet(at(y, lax.rem(z + d, NZ)), x)
    for d in range(1, NY):
        greet(at(lax.rem(y + d, NY), z), x)
    pl.semaphore_wait(barrier, 3 + (NZ - 1) + (NY - 1) + 2 * c)

    ex = [
        remote(k_hbm, kb.at[mine, :], ex_s.at[0], ex_r.at[0], sib, x),
        remote(v_hbm.at[:, sib_lanes], vb.at[mine, :], ex_s.at[1], ex_r.at[1], sib, x),
        remote(q_hbm, qb.at[c], ex_s.at[2], ex_r.at[2], sib, x),
    ]
    last = pl.ds(TOK - HALO, HALO)
    halos = []
    for cc in range(2):
        halos.append(
            remote(k_hbm.at[last, :], kb.at[0:HALO, :], halo_s.at[cc], halo_r.at[0], after * 2 + cc, x)
        )
        halos.append(
            remote(
                v_hbm.at[last, 256 * cc : 256 * cc + 256], vb.at[0:HALO, :],
                halo_s.at[2 + cc], halo_r.at[1], after * 2 + cc, x,
            )
        )

    @pl.when(c == 1)
    def _():
        for copy in halos:
            copy.start()

    for copy in ex:
        copy.start()
    ag_right = remote(cot_hbm, cotg.at[x], ag_s.at[0], ag_r.at[0], ctx, right)
    ag_left = remote(cot_hbm, cotg.at[x], ag_s.at[1], ag_r.at[1], ctx, left)
    ag_right.start()
    ag_left.start()

    load_k.wait()
    load_v.wait()
    load_q.wait()
    for copy in ex:
        copy.wait_recv()
    halos[0].wait_recv()
    halos[1].wait_recv()

    @pl.when(chip == 0)
    def _():
        kb[0:HALO, :] = jnp.zeros((HALO, kb.shape[1]), BF)
        vb[0:HALO, :] = jnp.zeros((HALO, vb.shape[1]), BF)

    def convolve(joined, taps):
        out = taps[0:1] * joined[HALO:]
        for j in range(1, CONV):
            out = out + taps[j : j + 1] * pltpu.roll(joined, j, 0)[HALO:]
        return out

    vc[...] = convolve(vb[...].astype(F32), cv_ref[:, own_lanes]).astype(BF)
    key_conv = convolve(kb[...].astype(F32), ck_ref[...])
    queries = jnp.concatenate([qb[0], qb[1]], 0).astype(F32)
    raw[...] = jnp.concatenate([queries, key_conv], 1).T
    heads_row = pl.multiple_of(32 * c, 32)
    for j in range(2):
        build_features(raw, 64 + heads_row + 16 * j, False, feat)
        k_pt[j] = feat[...].astype(BF)
        k_tp[j] = feat[...].T.astype(BF)
        lanes = slice(VDIM * j, VDIM * j + VDIM)
        s0 = mm(k_pt[j, :, 0:TOK], vc[0:TOK, lanes])
        state0[:, lanes] = s0
        a1[:, lanes] = (s0 + mm(k_pt[j, :, TOK:], vc[TOK:, lanes])).astype(BF)
    pick = lax.broadcasted_iota(jnp.int32, (8, 2 * TOK), 0)
    token = lax.broadcasted_iota(jnp.int32, (8, 2 * TOK), 1)
    norms = jnp.zeros((8, ROWS), F32)
    for j in range(2):
        chosen = (pick == j) | ((pick == 2 + j) & (token < TOK))
        norms = norms + mm(jnp.where(chosen, 1.0, 0.0).astype(BF), k_tp[j])
    n1[...] = jnp.zeros(n1.shape, F32)
    n1[:, 0:ROWS] = norms

    def group(ref, g):
        return ref.at[pl.ds(pl.multiple_of(16 * g, 16), 16), :]

    def spread(source, landing, sends, recvs, with_norm):
        for d in range(1, NZ):
            to = lax.rem(z + d, NZ)

            @pl.when(to < GROUPS)
            def _():
                remote(
                    group(source, to), landing.at[z], sends.at[d], recvs.at[z], at(y, to), x
                ).start()

            if with_norm:

                @pl.when(to == NORM)
                def _():
                    remote(n1, rn.at[z], sends.at[d], recvs.at[z], at(y, to), x).start()

    def spread_end(source, landing, sends, recvs, with_norm):
        for d in range(1, NZ):
            to = lax.rem(z + d, NZ)

            @pl.when(to < GROUPS)
            def _():
                remote(
                    group(source, to), landing.at[z], sends.at[d], recvs.at[z], at(y, to), x
                ).wait_send()

            if with_norm:

                @pl.when(to == NORM)
                def _():
                    remote(n1, rn.at[z], sends.at[d], recvs.at[z], at(y, to), x).wait_send()

    def sum_up(source, landing, recvs, sums, ys, yr, landing_y, forward):
        landing[z] = source
        for d in range(1, NZ):
            frm = lax.rem(z + d, NZ)
            remote(sums, landing.at[frm], ys.at[0], recvs.at[frm], ctx, x).wait_recv()
        acc = landing[0].astype(F32)
        for j in range(1, NZ):
            acc = acc + landing[j].astype(F32)
        sums[...] = acc.astype(sums.dtype)
        for d in range(1, NY):
            to = y + d if forward else y - d
            need = to < NY if forward else to >= 0

            @pl.when(need)
            def _():
                remote(sums, landing_y.at[y], ys.at[d], yr.at[y], at(to, z), x).start()

    def hand_out(landing, sums, ys, yr, landing_y, start, outs, forward, send_one, keep_own):
        start[...] = jnp.zeros(start.shape, F32)
        for d in range(1, NY):
            frm = y - d if forward else y + d
            there = frm >= 0 if forward else frm < NY

            @pl.when(there)
            def _():
                remote(sums, landing_y.at[frm], ys.at[0], yr.at[frm], ctx, x).wait_recv()
                start[...] += landing_y[frm].astype(F32)

        run = start[...]
        order = range(NZ) if forward else range(NZ - 1, -1, -1)
        for j in order:
            outs[j] = run.astype(outs.dtype)
            run = run + landing[j].astype(F32)
        for d in range(1, NZ):
            send_one(d, lax.rem(z + d, NZ)).start()
        keep_own(outs[z])

    def y_end(sums, ys, yr, landing_y, forward):
        for d in range(1, NY):
            to = y + d if forward else y - d
            need = to < NY if forward else to >= 0

            @pl.when(need)
            def _():
                remote(sums, landing_y.at[y], ys.at[d], yr.at[y], at(to, z), x).wait_send()

    spread(a1, r1, p1_s, p1_r, True)

    for j in range(2):
        build_features(raw, heads_row + 16 * j, True, feat)
        q_pt[j] = feat[...].astype(BF)
        q_tp[j] = feat[...].T.astype(BF)
    t_at = lax.broadcasted_iota(jnp.int32, (TOK, TOK), 0)
    s_at = lax.broadcasted_iota(jnp.int32, (TOK, TOK), 1)
    for j in range(2):
        for b in range(2):
            rows = slice(TOK * b, TOK * b + TOK)
            scores = jnp.where(t_at >= s_at, mm(q_tp[j, rows], k_pt[j, :, rows]), 0.0)
            wl[j, b] = scores.astype(BF)
            dsum[j, rows] = jnp.sum(scores, 1, keepdims=True)

    @pl.when(z < GROUPS)
    def _():
        sum_up(group(a1, z)[...], r1, p1_r, tsum, y_s, y_r, ry, True)

    @pl.when(z == NORM)
    def _():
        sum_up(n1[...], rn, p1_r, tnorm, y_s, y_r, ryn, True)

    upper, lower = slice(0, TOK // 2), slice(TOK // 2, TOK)
    ag_right.wait_recv()
    ag2_right = remote(
        cotg.at[left, upper], cotg.at[left, upper], ag_s.at[2], ag_r.at[2], ctx, right
    )
    ag2_right.start()
    ag_left.wait_recv()
    ag2_left = remote(
        cotg.at[right, lower], cotg.at[right, lower], ag_s.at[3], ag_r.at[3], ctx, left
    )
    ag2_left.start()

    for j in range(2):
        for b in range(2):
            rows = slice(TOK * b, TOK * b + TOK)
            flipped = jnp.where(s_at >= t_at, mm(k_tp[j, rows], q_pt[j, :, rows]), 0.0)
            wlt[j, b] = flipped.astype(BF)

    def out_state(d, to):
        return remote(qo.at[to], group(pr, z), p3_s.at[d], p3_r.at[z], at(y, to), x)

    def out_norm(d, to):
        return remote(qn.at[to], pn, p3_s.at[d], p3_r.at[z], at(y, to), x)

    def keep_state(value):
        group(pr, z)[...] = value

    def keep_norm(value):
        pn[...] = value

    @pl.when(z < GROUPS)
    def _():
        hand_out(r1, tsum, y_s, y_r, ry, base, qo, True, out_state, keep_state)

    @pl.when(z == NORM)
    def _():
        hand_out(rn, tnorm, y_s, y_r, ryn, basen, qn, True, out_norm, keep_norm)

    load_w.wait()
    load_c.wait()
    remote(cotg.at[far, upper], cotg.at[far, upper], ag_s.at[2], ag_r.at[2], ctx, right).wait_recv()
    remote(cotg.at[far, lower], cotg.at[far, lower], ag_s.at[3], ag_r.at[3], ctx, left).wait_recv()

    def out_grad(row0):
        acc = None
        for i in range(NX):
            part = mm_t(cotg[i], w[pl.ds(row0, 256), 512 * i : 512 * i + 512])
            acc = part if acc is None else acc + part
        return acc

    ogs[...] = out_grad(pl.multiple_of(256 * (1 - c), 256))
    og_copy = remote(ogs, og.at[c], misc_s.at[0], misc_r.at[0], sib, x)
    og_copy.start()
    og[c] = out_grad(pl.multiple_of(256 * c, 256))

    for j in range(GROUPS):

        @pl.when(z != j)
        def _():
            remote(qo.at[0], pr.at[16 * j : 16 * j + 16, :], p3_s.at[0], p3_r.at[j], ctx, x).wait_recv()

    @pl.when(z != NORM)
    def _():
        remote(qn.at[0], pn, p3_s.at[0], p3_r.at[NORM], ctx, x).wait_recv()

    og_copy.wait_recv()
    for b in range(2):
        rows = slice(TOK * b, TOK * b + TOK)
        for j in range(2):
            lanes = slice(VDIM * j, VDIM * j + VDIM)
            norm = pn[j : j + 1, 0:ROWS]
            if b == 1:
                norm = norm + n1[2 + j : 3 + j, 0:ROWS]
            there = jnp.sum(q_tp[j, rows].astype(F32) * norm, 1, keepdims=True)
            inverse = 1.0 / (dsum[j, rows] + there)
            dsum[j, rows] = inverse
            grad[rows, lanes] = (og[b, :, lanes] * inverse).astype(BF)
    for j in range(2):
        lanes = slice(VDIM * j, VDIM * j + VDIM)
        later = mm(q_pt[j, :, TOK:], grad[TOK:, lanes])
        u1[:, lanes] = later
        a2[:, lanes] = (later + mm(q_pt[j, :, 0:TOK], grad[0:TOK, lanes])).astype(BF)
    spread(a2, r2, g1_s, g1_r, False)

    total[...] = (pr[...].astype(F32) + state0[...]).astype(BF)
    for b in range(2):
        rows = slice(TOK * b, TOK * b + TOK)
        prior = pr if b == 0 else total
        parts = []
        for j in range(2):
            lanes = slice(VDIM * j, VDIM * j + VDIM)
            numerator = mm(wl[j, b], vc[rows, lanes]) + mm(q_tp[j, rows], prior[:, lanes])
            parts.append((numerator * dsum[j, rows]).astype(BF))
        atts[b] = jnp.concatenate(parts, 1)
    at_copy = remote(atts.at[1 - c], att.at[c], misc_s.at[1], misc_r.at[1], sib, x)
    at_copy.start()
    att[c] = atts[c]

    @pl.when(z < GROUPS)
    def _():
        sum_up(group(a2, z)[...], r2, g1_r, t2, gy_s, gy_r, ry2, False)

    at_copy.wait_recv()

    def project(to):
        columns = pl.ds(pl.multiple_of(512 * to, 512), 512)
        return mm(att[0], w[0:256, columns]) + mm(att[1], w[256:512, columns])

    part = project(far)
    rs1s[0] = part[upper].astype(BF)
    rs1s[1] = part[lower].astype(BF)
    rs1 = [
        remote(rs1s.at[0], rs1r.at[0], rs_s.at[0], rs_r.at[0], ctx, right),
        remote(rs1s.at[1], rs1r.at[1], rs_s.at[1], rs_r.at[1], ctx, left),
    ]
    rs1[0].start()
    rs1[1].start()

    def out_later(d, to):
        return remote(qo2.at[to], group(pr2, z), g3_s.at[d], g3_r.at[z], at(y, to), x)

    def keep_later(value):
        group(pr2, z)[...] = value

    @pl.when(z < GROUPS)
    def _():
        hand_out(r2, t2, gy_s, gy_r, ry2, base, qo2, False, out_later, keep_later)

    to_right = project(right)
    to_left = project(left)
    rs1[0].wait_recv()
    rs2s[0, upper] = (to_right[upper] + rs1r[0].astype(F32)).astype(BF)
    rs2s[0, lower] = to_right[lower].astype(BF)
    rs2_right = remote(rs2s.at[0], rs2r.at[0], rs_s.at[2], rs_r.at[2], ctx, right)
    rs2_right.start()
    rs1[1].wait_recv()
    rs2s[1, lower] = (to_left[lower] + rs1r[1].astype(F32)).astype(BF)
    rs2s[1, upper] = to_left[upper].astype(BF)
    rs2_left = remote(rs2s.at[1], rs2r.at[1], rs_s.at[3], rs_r.at[3], ctx, left)
    rs2_left.start()
    here = project(x)

    for j in range(GROUPS):

        @pl.when(z != j)
        def _():
            remote(qo2.at[0], pr2.at[16 * j : 16 * j + 16, :], g3_s.at[0], g3_r.at[j], ctx, x).wait_recv()

    total[...] = (pr2[...].astype(F32) + u1[...]).astype(BF)
    for b in range(2):
        rows = slice(TOK * b, TOK * b + TOK)
        later = total if b == 0 else pr2
        parts = []
        for j in range(2):
            lanes = slice(VDIM * j, VDIM * j + VDIM)
            value = mm(wlt[j, b], grad[rows, lanes]) + mm(k_tp[j, rows], later[:, lanes])
            parts.append(value.astype(BF))
        vgs[b] = jnp.concatenate(parts, 1)
    vg_copy = remote(vgs.at[1 - c], vgrad_ref.at[:, own_lanes], misc_s.at[2], misc_r.at[2], sib, x)
    vg_copy.start()
    vgrad_ref[:, own_lanes] = vgs[c]

    rs2_right.wait_recv()
    rs2_left.wait_recv()
    mixed_ref[...] = (here + rs2r[0].astype(F32) + rs2r[1].astype(F32)).astype(BF)

    for copy in ex:
        copy.wait_send()

    @pl.when(c == 1)
    def _():
        for copy in halos:
            copy.wait_send()

    for copy in (ag_right, ag_left, ag2_right, ag2_left, og_copy, at_copy, rs1[0], rs1[1], rs2_right, rs2_left):
        copy.wait_send()
    spread_end(a1, r1, p1_s, p1_r, True)
    spread_end(a2, r2, g1_s, g1_r, False)

    @pl.when(z < GROUPS)
    def _():
        y_end(tsum, y_s, y_r, ry, True)
        y_end(t2, gy_s, gy_r, ry2, False)
        for d in range(1, NZ):
            out_state(d, lax.rem(z + d, NZ)).wait_send()
            out_later(d, lax.rem(z + d, NZ)).wait_send()

    @pl.when(z == NORM)
    def _():
        y_end(tnorm, y_s, y_r, ryn, True)
        for d in range(1, NZ):
            out_norm(d, lax.rem(z + d, NZ)).wait_send()

    vg_copy.wait_send()
    vg_copy.wait_recv()


def per_device(queries, keys, values, conv_keys, conv_values, out_weight, cotangent):
    vmem = pltpu.VMEM
    dma = pltpu.SemaphoreType.DMA
    both = 2 * TOK
    scratch = [
        vmem((2, TOK, 64), BF),
        vmem((HALO + both, 64), BF),
        vmem((HALO + both, 256), BF),
        vmem((512, 2048), BF),
        vmem((NX, TOK, 512), BF),
        vmem((128, both), F32),
        vmem((ROWS, both), F32),
        vmem((2, ROWS, both), BF),
        vmem((2, both, ROWS), BF),
        vmem((2, ROWS, both), BF),
        vmem((2, both, ROWS), BF),
        vmem((both, 256), BF),
        vmem((2, 2, TOK, TOK), BF),
        vmem((2, 2, TOK, TOK), BF),
        vmem((2, both, 1), F32),
        vmem((ROWS, 256), F32),
        vmem((ROWS, 256), BF),
        vmem((ROWS, 256), BF),
        vmem((8, 256), F32),
        vmem((NZ, 16, 256), BF),
        vmem((NZ, 8, 256), F32),
        vmem((16, 256), BF),
        vmem((8, 256), F32),
        vmem((NY, 16, 256), BF),
        vmem((NY, 8, 256), F32),
        vmem((16, 256), F32),
        vmem((8, 256), F32),
        vmem((NZ, 16, 256), BF),
        vmem((NZ, 8, 256), F32),
        vmem((ROWS, 256), BF),
        vmem((8, 256), F32),
        vmem((2, TOK, 256), F32),
        vmem((TOK, 256), F32),
        vmem((both, 256), BF),
        vmem((ROWS, 256), F32),
        vmem((ROWS, 256), BF),
        vmem((NZ, 16, 256), BF),
        vmem((16, 256), BF),
        vmem((NY, 16, 256), BF),
        vmem((NZ, 16, 256), BF),
        vmem((ROWS, 256), BF),
        vmem((2, TOK, 256), BF),
        vmem((2, TOK, 256), BF),
        vmem((2, TOK, 256), BF),
        vmem((2, TOK // 2, 512), BF),
        vmem((2, TOK // 2, 512), BF),
        vmem((2, TOK, 512), BF),
        vmem((2, TOK, 512), BF),
        dma((5,)),
        dma((3,)), dma((3,)),
        dma((4,)), dma((2,)),
        dma((NZ,)), dma((NZ,)), dma((NY,)), dma((NY,)), dma((NZ,)), dma((NZ,)),
        dma((NZ,)), dma((NZ,)), dma((NY,)), dma((NY,)), dma((NZ,)), dma((NZ,)),
        dma((4,)), dma((4,)), dma((4,)), dma((4,)), dma((3,)), dma((3,)),
    ]
    in_hbm = pl.BlockSpec(memory_space=pl.ANY)
    in_vmem = pl.BlockSpec(memory_space=pltpu.VMEM)
    out = jax.ShapeDtypeStruct(values.shape, BF)
    return pl.pallas_call(
        body,
        out_shape=(out, out),
        in_specs=[in_hbm, in_hbm, in_hbm, in_vmem, in_vmem, in_hbm, in_hbm],
        out_specs=(in_vmem, in_vmem),
        scratch_shapes=scratch,
        compiler_params=pltpu.CompilerParams(
            collective_id=0, has_side_effects=True, vmem_limit_bytes=48 << 20
        ),
    )(queries, keys, values, conv_keys, conv_values, out_weight, cotangent)


def solution(mesh):
    in_specs = (
        P("ctx", "head"),
        P("ctx", "head"),
        P("ctx", "head"),
        P(None, "head"),
        P(None, "head"),
        P("head", None),
        P("ctx", "head"),
    )
    out_specs = (P("ctx", "head"), P("ctx", "head"))
    return jax.shard_map(
        per_device, mesh=mesh, in_specs=in_specs, out_specs=out_specs, check_vma=False
    )
```

```python
import functools

import jax
import jax.numpy as jnp
from jax import lax
from jax.experimental import pallas as pl
from jax.experimental.pallas import tpu as pltpu
from jax.sharding import PartitionSpec as P

FEAT = 16
VDIM = 128
CONV = 3
NY, NZ, NX = 8, 12, 4
TOK = 256
ROWS = 160
GROUPS = ROWS // 16
HALO = 16
ALONG_Z = sorted(range(1, NZ), key=lambda d: -min(d, NZ - d))
ALONG_Y = sorted(range(1, NY), key=lambda d: -min(d, NY - d))
BF = jnp.bfloat16
F32 = jnp.float32


def mm(a, b):
    return jnp.dot(a, b, preferred_element_type=F32)


def mm_t(a, b):
    return lax.dot_general(a, b, (((1,), (1,)), ((), ())), preferred_element_type=F32)


def remote(src, dst, send, recv, ctx, head):
    return pltpu.make_async_remote_copy(
        src_ref=src,
        dst_ref=dst,
        send_sem=send,
        recv_sem=recv,
        device_id=(ctx, head),
        device_id_type=pl.DeviceIdType.MESH,
    )


def build_features(channels, query, store):
    s = channels * FEAT ** (-0.25)
    half = 0.5**0.5
    pair = 2.0 * half if query else half
    store[0:16, :] = s * s * half
    for d in range(1, 8):
        store[16 * d : 16 * d + 16, :] = s * pltpu.roll(s, FEAT - d, 0) * pair
    store[128:136, :] = s[0:8] * s[8:16] * pair
    row = lax.broadcasted_iota(jnp.int32, (8, s.shape[1]), 0)
    store[136:144, :] = jnp.where(row == 0, 1.0, 0.0)
    store[144:160, :] = s


def body(
    q_hbm, k_hbm, v_hbm, ck_hbm, cv_hbm, w_hbm, cot_hbm, mixed_ref, vgrad_ref,
    ck, cv, taps, qb, kb, vb, w, cotg, feat, q_pt, q_tp, k_pt, k_tp, vc, wl, dsum,
    state0, total, a1, n1, own0, nz, nt, ny, r1, tsum, ry, base, qo, pr,
    og, ogs, grad, vin, u1, a2, r2, t2, ry2, qo2, pr2, atts, vgs,
    attg, wcol,
    loc, ex_s, ex_r, halo_s, halo_r, p1_s, p1_r, y_s, y_r, p3_s, p3_r,
    g1_s, g1_r, gy_s, gy_r, g3_s, g3_r, ag_s, ag_r, nz_s, nz_r, ny_s, ny_r, wc_s, wc_r, wf_s, wf_r, at_s, at_r, misc_s, misc_r,
):
    ctx = lax.axis_index("ctx")
    x = lax.axis_index("head")
    y = lax.div(ctx, 2 * NZ)
    chip = lax.div(ctx, 2)
    z = lax.rem(chip, NZ)
    c = lax.rem(ctx, 2)
    sib = chip * 2 + 1 - c
    chips = NY * NZ
    before = lax.rem(chip + chips - 1, chips)
    after = lax.rem(chip + 1, chips)
    right, left = lax.rem(x + 1, NX), lax.rem(x + NX - 1, NX)
    far = lax.rem(x + 2, NX)

    def at(y_, z_):
        return (y_ * NZ + z_) * 2 + c

    sent, due = [], {}

    def go(copy, name=None):
        copy.start()
        sent.append(copy.wait_send)
        if name is not None:
            due[name] = copy.wait_recv
        return copy

    def arrived(name):
        due.pop(name)()

    def finish():
        for name in list(due):
            arrived(name)
        for wait in sent:
            wait()

    own_lanes = pl.ds(pl.multiple_of(256 * c, 256), 256)
    sib_lanes = pl.ds(pl.multiple_of(256 * (1 - c), 256), 256)
    own_rows = pl.ds(pl.multiple_of(32 * c, 32), 32)
    sib_rows = pl.ds(pl.multiple_of(32 * (1 - c), 32), 32)
    mine = pl.ds(pl.multiple_of(HALO + TOK * c, 16), TOK)
    mine_k = pl.ds(pl.multiple_of(128 + TOK * c, 128), TOK)
    loads = [
        pltpu.make_async_copy(ck_hbm, ck, loc.at[5]),
        pltpu.make_async_copy(cv_hbm.at[:, own_lanes], cv, loc.at[6]),
        pltpu.make_async_copy(k_hbm.at[own_rows, :], kb.at[:, mine_k], loc.at[1]),
        pltpu.make_async_copy(q_hbm.at[own_rows, :], qb.at[:, own_lanes], loc.at[3]),
        pltpu.make_async_copy(v_hbm.at[:, own_lanes], vb.at[mine, :], loc.at[2]),
    ]
    for copy in loads:
        copy.start()
    load_c = pltpu.make_async_copy(cot_hbm, cotg.at[x], loc.at[4])
    load_w = pltpu.make_async_copy(w_hbm, w, loc.at[0])
    load_c.start()
    load_w.start()
    due["c"] = load_c.wait
    due["w"] = load_w.wait

    barrier = pltpu.get_barrier_semaphore()

    def greet(ctx_, x_):
        pl.semaphore_signal(
            barrier, inc=1, device_id=(ctx_, x_), device_id_type=pl.DeviceIdType.MESH
        )

    for d in ALONG_Z:
        greet(at(y, lax.rem(z + d, NZ)), x)
    for d in ALONG_Y:
        greet(at(lax.rem(y + d, NY), z), x)
    greet(ctx, far)
    greet(before * 2 + 1, x)
    greet(ctx, right)
    greet(ctx, left)
    greet(sib, x)
    pl.semaphore_wait(barrier, 4 + (NZ - 1) + (NY - 1) + 2 * c)

    last = pl.ds(TOK - HALO, HALO)
    halos = []
    for cc in range(2):
        halos.append(
            remote(
                k_hbm.at[32 * cc : 32 * cc + 32, TOK - 128 : TOK], kb.at[:, 0:128],
                halo_s.at[cc], halo_r.at[0], after * 2 + cc, x,
            )
        )
        halos.append(
            remote(
                v_hbm.at[last, 256 * cc : 256 * cc + 256], vb.at[0:HALO, :],
                halo_s.at[2 + cc], halo_r.at[1], after * 2 + cc, x,
            )
        )

    @pl.when(c == 1)
    def _():
        for copy in halos:
            copy.start()

    def halos_left():
        @pl.when(c == 1)
        def _():
            for copy in halos:
                copy.wait_send()

    sent.append(halos_left)
    due["halo_k"] = halos[0].wait_recv
    due["halo_v"] = halos[1].wait_recv
    go(remote(k_hbm.at[sib_rows, :], kb.at[:, mine_k], ex_s.at[0], ex_r.at[0], sib, x), "k")
    go(remote(v_hbm.at[:, sib_lanes], vb.at[mine, :], ex_s.at[1], ex_r.at[1], sib, x), "v")
    go(remote(q_hbm.at[sib_rows, :], qb.at[:, own_lanes], ex_s.at[2], ex_r.at[2], sib, x), "q")
    def gather(own, slots, sends, recvs, name):
        go(remote(own(0), slots(x, 0), sends.at[0], recvs.at[0], ctx, right), name + "_left0")
        go(remote(own(1), slots(x, 1), sends.at[1], recvs.at[1], ctx, left), name + "_right1")
        go(remote(own(1), slots(x, 1), sends.at[2], recvs.at[2], ctx, right), name + "_left1")
        go(remote(own(0), slots(x, 0), sends.at[3], recvs.at[3], ctx, left), name + "_right0")

    def pass_on(slots, sends, recvs, name):
        arrived(name + "_left0")
        go(remote(slots(left, 0), slots(left, 0), sends.at[4], recvs.at[4], ctx, right), name + "_far0")
        arrived(name + "_right1")
        go(remote(slots(right, 1), slots(right, 1), sends.at[5], recvs.at[5], ctx, left), name + "_far1")

    cot_half = lambda i: pl.ds(TOK // 2 * i, TOK // 2)
    cot_slot = lambda who, i: cotg.at[who, cot_half(i)]
    gather(lambda i: cot_hbm.at[cot_half(i), :], cot_slot, ag_s, ag_r, "cot")

    for copy in loads:
        copy.wait()
    for name in ("k", "halo_k", "v", "halo_v"):
        arrived(name)

    @pl.when(chip == 0)
    def _():
        kb[:, 0:128] = jnp.zeros((32, 128), BF)
        vb[0:HALO, :] = jnp.zeros((HALO, 256), BF)

    taps[...] = jnp.zeros(taps.shape, F32)
    taps[0:CONV, 0:64] = ck[...]
    taps[...] = taps[...].T
    tap = taps[own_rows, :]
    joined = kb[...].astype(F32)
    key_conv = tap[:, 0:1] * joined[:, 128:]
    for j in range(1, CONV):
        key_conv = key_conv + tap[:, j : j + 1] * pltpu.roll(joined, j, 1)[:, 128:]
    for j in range(2):
        build_features(key_conv[16 * j : 16 * j + 16], False, feat)
        k_pt[j] = feat[...].astype(BF)
        k_tp[j] = feat[...].T.astype(BF)
    pick = lax.broadcasted_iota(jnp.int32, (8, 2 * TOK), 0)
    token = lax.broadcasted_iota(jnp.int32, (8, 2 * TOK), 1)
    ones = jnp.where((pick == 0) | ((pick == 1) & (token < TOK)), 1.0, 0.0).astype(BF)
    n1[...] = jnp.zeros(n1.shape, F32)
    for j in range(2):
        norms = mm(ones, k_tp[j])
        n1[2 * j : 2 * j + 1, :] = norms[0:1, 0:128]
        n1[2 * j + 1 : 2 * j + 2, 0 : ROWS - 128] = norms[0:1, 128:]
        own0[j] = norms
    for d in ALONG_Z:
        to = lax.rem(z + d, NZ)
        go(remote(n1, nz.at[z], nz_s.at[d], nz_r.at[z], at(y, to), x))
    nz[z] = n1[...]

    joined = vb[...].astype(F32)
    value_conv = cv[0:1] * joined[HALO:]
    for j in range(1, CONV):
        value_conv = value_conv + cv[j : j + 1] * pltpu.roll(joined, j, 0)[HALO:]
    vc[...] = value_conv.astype(BF)
    for j in range(2):
        lanes = slice(VDIM * j, VDIM * j + VDIM)
        s0 = mm(k_pt[j, :, 0:TOK], vc[0:TOK, lanes])
        state0[:, lanes] = s0
        a1[:, lanes] = (s0 + mm(k_pt[j, :, TOK:], vc[TOK:, lanes])).astype(BF)

    def group(ref, g):
        return ref.at[pl.ds(pl.multiple_of(16 * g, 16), 16), :]

    def spread(source, landing, sends, recvs):
        for d in ALONG_Z:
            to = lax.rem(z + d, NZ)

            @pl.when(to < GROUPS)
            def _():
                remote(
                    group(source, to), landing.at[z], sends.at[d], recvs.at[z], at(y, to), x
                ).start()

    def spread_end(source, landing, sends, recvs):
        for d in ALONG_Z:
            to = lax.rem(z + d, NZ)

            @pl.when(to < GROUPS)
            def _():
                remote(
                    group(source, to), landing.at[z], sends.at[d], recvs.at[z], at(y, to), x
                ).wait_send()

    def sum_up(source, source_like, landing, recvs, sums, ys, yr, landing_y, forward):
        landing[z] = source
        for d in ALONG_Z:
            frm = lax.rem(z + d, NZ)
            remote(source_like, landing.at[frm], ys.at[0], recvs.at[frm], ctx, x).wait_recv()
        acc = landing[0].astype(F32)
        for j in range(1, NZ):
            acc = acc + landing[j].astype(F32)
        sums[...] = acc.astype(sums.dtype)
        for d in ALONG_Y:
            to = y + d if forward else y - d
            need = to < NY if forward else to >= 0

            @pl.when(need)
            def _():
                remote(sums, landing_y.at[y], ys.at[d], yr.at[y], at(to, z), x).start()

    def hand_out(landing, sums, ys, yr, landing_y, start, outs, forward, send_one, keep_own):
        start[...] = jnp.zeros(start.shape, F32)
        for d in ALONG_Y:
            frm = y - d if forward else y + d
            there = frm >= 0 if forward else frm < NY

            @pl.when(there)
            def _():
                remote(sums, landing_y.at[frm], ys.at[0], yr.at[frm], ctx, x).wait_recv()
                start[...] += landing_y[frm].astype(F32)

        run = start[...]
        order = range(NZ) if forward else range(NZ - 1, -1, -1)
        for j in order:
            outs[j] = run.astype(outs.dtype)
            run = run + landing[j].astype(F32)
        for d in ALONG_Z:
            send_one(d, lax.rem(z + d, NZ)).start()
        keep_own(outs[z])

    def y_end(sums, ys, yr, landing_y, forward):
        for d in ALONG_Y:
            to = y + d if forward else y - d
            need = to < NY if forward else to >= 0

            @pl.when(need)
            def _():
                remote(sums, landing_y.at[y], ys.at[d], yr.at[y], at(to, z), x).wait_send()

    spread(a1, r1, p1_s, p1_r)
    sent.append(lambda: spread_end(a1, r1, p1_s, p1_r))

    arrived("q")
    for j in range(2):
        build_features(qb[16 * j : 16 * j + 16, :].astype(F32), True, feat)
        q_pt[j] = feat[...].astype(BF)
        q_tp[j] = feat[...].T.astype(BF)
    t_at = lax.broadcasted_iota(jnp.int32, (TOK, TOK), 0)
    s_at = lax.broadcasted_iota(jnp.int32, (TOK, TOK), 1)
    for j in range(2):
        for b in range(2):
            rows = slice(TOK * b, TOK * b + TOK)
            scores = jnp.where(t_at >= s_at, mm(q_tp[j, rows], k_pt[j, :, rows]), 0.0)
            wl[j, b] = scores.astype(BF)
            dsum[j, rows] = jnp.sum(scores, 1, keepdims=True)

    pass_on(cot_slot, ag_s, ag_r, "cot")

    for d in ALONG_Z:
        frm = lax.rem(z + d, NZ)
        remote(n1, nz.at[frm], nz_s.at[0], nz_r.at[frm], ctx, x).wait_recv()
    acc = nz[0]
    for j in range(1, NZ):
        acc = acc + nz[j]
    nt[...] = acc
    for d in ALONG_Y:

        @pl.when(y + d < NY)
        def _():
            remote(nt, ny.at[y], ny_s.at[d], ny_r.at[y], at(y + d, z), x).start()

    def norms_left():
        for d in ALONG_Y:

            @pl.when(y + d < NY)
            def _():
                remote(nt, ny.at[y], ny_s.at[d], ny_r.at[y], at(y + d, z), x).wait_send()

    sent.append(norms_left)

    half = pl.ds(pl.multiple_of(256 * c, 256), 256)
    for d in (1, 3, 2):
        to = lax.rem(x + d, NX)
        columns = pl.ds(pl.multiple_of(512 * to, 512), 512)
        go(remote(w_hbm.at[half, columns], wcol.at[x, half], wc_s.at[d], wc_r.at[d], ctx, to))
    load_wc = pltpu.make_async_copy(
        w_hbm.at[:, pl.ds(pl.multiple_of(512 * x, 512), 512)], wcol.at[x], loc.at[7]
    )
    load_wc.start()

    arrived("c")
    arrived("w")

    def out_grad(who, row0):
        columns = pl.ds(pl.multiple_of(512 * who, 512), 512)
        return mm_t(cotg[who], w[pl.ds(row0, 256), columns])

    own_row = pl.multiple_of(256 * c, 256)
    sib_row = pl.multiple_of(256 * (1 - c), 256)
    for name in ("cot_left1", "cot_right0"):
        arrived(name)
    ogs[...] = out_grad(x, sib_row) + out_grad(left, sib_row) + out_grad(right, sib_row)
    og[c] = out_grad(x, own_row) + out_grad(left, own_row) + out_grad(right, own_row)

    @pl.when(z < GROUPS)
    def _():
        sum_up(group(a1, z)[...], group(a1, z), r1, p1_r, tsum, y_s, y_r, ry, True)

    arrived("cot_far0")
    arrived("cot_far1")
    ogs[...] += out_grad(far, sib_row)
    go(remote(ogs, og.at[c], misc_s.at[0], misc_r.at[0], sib, x), "og")
    og[c] += out_grad(far, own_row)

    base_n = jnp.zeros((4, 128), F32)
    for j in range(NZ):
        base_n = base_n + jnp.where(j < z, nz[j], 0.0)
    for j in range(NY):

        @pl.when(j >= y)
        def _():
            ny[j] = jnp.zeros((4, 128), F32)

        @pl.when(j < y)
        def _():
            remote(nt, ny.at[j], ny_s.at[0], ny_r.at[j], ctx, x).wait_recv()

    for j in range(NY):
        base_n = base_n + ny[j]
    arrived("og")
    for b in range(2):
        rows = slice(TOK * b, TOK * b + TOK)
        for j in range(2):
            lanes = slice(VDIM * j, VDIM * j + VDIM)
            norm = jnp.concatenate(
                [base_n[2 * j : 2 * j + 1], base_n[2 * j + 1 : 2 * j + 2, 0 : ROWS - 128]], 1
            )
            if b == 1:
                norm = norm + own0[j, 1:2]
            there = jnp.sum(q_tp[j, rows].astype(F32) * norm, 1, keepdims=True)
            inverse = 1.0 / (dsum[j, rows] + there)
            dsum[j, rows] = inverse
            grad[rows, lanes] = (og[b, :, lanes] * inverse).astype(BF)
    for j in range(2):
        lanes = slice(VDIM * j, VDIM * j + VDIM)
        later = mm(q_pt[j, :, TOK:], grad[TOK:, lanes])
        u1[:, lanes] = later
        a2[:, lanes] = (later + mm(q_pt[j, :, 0:TOK], grad[0:TOK, lanes])).astype(BF)
    spread(a2, r2, g1_s, g1_r)
    sent.append(lambda: spread_end(a2, r2, g1_s, g1_r))

    def out_state(d, to):
        return remote(qo.at[to], group(pr, z), p3_s.at[d], p3_r.at[z], at(y, to), x)

    def keep_state(value):
        group(pr, z)[...] = value

    @pl.when(z < GROUPS)
    def _():
        hand_out(r1, tsum, y_s, y_r, ry, base, qo, True, out_state, keep_state)

    for d in (1, 3, 2):
        frm = lax.rem(x + NX - d, NX)
        remote(
            w_hbm.at[half, 0:512], wcol.at[frm, half], wc_s.at[d], wc_r.at[d], ctx, x
        ).wait_recv()
        go(
            remote(wcol.at[frm, half], wcol.at[frm, half], wf_s.at[d], wf_r.at[d], sib, x),
            "wcol%d" % d,
        )

    for j in range(2):
        lanes = slice(VDIM * j, VDIM * j + VDIM)
        for b in range(2):
            rows = slice(TOK * b, TOK * b + TOK)
            flipped = jnp.where(s_at >= t_at, mm(k_tp[j, rows], q_pt[j, :, rows]), 0.0)
            vin[rows, lanes] = mm(flipped.astype(BF), grad[rows, lanes])

    @pl.when(z < GROUPS)
    def _():
        sum_up(group(a2, z)[...], group(a2, z), r2, g1_r, t2, gy_s, gy_r, ry2, False)

    for j in range(GROUPS):

        @pl.when(z != j)
        def _():
            remote(
                qo.at[0], pr.at[16 * j : 16 * j + 16, :], p3_s.at[0], p3_r.at[j], ctx, x
            ).wait_recv()

    total[...] = (pr[...].astype(F32) + state0[...]).astype(BF)
    for b in range(2):
        rows = slice(TOK * b, TOK * b + TOK)
        prior = pr if b == 0 else total
        parts = []
        for j in range(2):
            lanes = slice(VDIM * j, VDIM * j + VDIM)
            numerator = mm(wl[j, b], vc[rows, lanes]) + mm(q_tp[j, rows], prior[:, lanes])
            parts.append((numerator * dsum[j, rows]).astype(BF))
        atts[b] = jnp.concatenate(parts, 1)
    go(remote(atts.at[1 - c], attg.at[x, c], misc_s.at[1], misc_r.at[1], sib, x), "att")
    attg[x, c] = atts[c]
    arrived("att")
    att_slot = lambda who, i: attg.at[who, i]
    gather(lambda i: attg.at[x, i], att_slot, at_s, at_r, "att")

    def out_later(d, to):
        return remote(qo2.at[to], group(pr2, z), g3_s.at[d], g3_r.at[z], at(y, to), x)

    def keep_later(value):
        group(pr2, z)[...] = value

    @pl.when(z < GROUPS)
    def _():
        hand_out(r2, t2, gy_s, gy_r, ry2, base, qo2, False, out_later, keep_later)

    load_wc.wait()
    for d in (1, 3, 2):
        arrived("wcol%d" % d)

    def project(frm):
        return mm(attg[frm, 0], wcol[frm, 0:256]) + mm(attg[frm, 1], wcol[frm, 256:512])

    mixed = project(x)
    pass_on(att_slot, at_s, at_r, "att")

    for j in range(GROUPS):

        @pl.when(z != j)
        def _():
            remote(
                qo2.at[0], pr2.at[16 * j : 16 * j + 16, :], g3_s.at[0], g3_r.at[j], ctx, x
            ).wait_recv()

    total[...] = (pr2[...].astype(F32) + u1[...]).astype(BF)
    for b in range(2):
        rows = slice(TOK * b, TOK * b + TOK)
        later = total if b == 0 else pr2
        parts = []
        for j in range(2):
            lanes = slice(VDIM * j, VDIM * j + VDIM)
            value = vin[rows, lanes] + mm(k_tp[j, rows], later[:, lanes])
            parts.append(value.astype(BF))
        vgs[b] = jnp.concatenate(parts, 1)
    go(
        remote(vgs.at[1 - c], vgrad_ref.at[:, own_lanes], misc_s.at[2], misc_r.at[2], sib, x),
        "value_grad",
    )
    vgrad_ref[:, own_lanes] = vgs[c]

    for who, name in ((left, "left"), (right, "right"), (far, "far")):
        arrived("att_" + name + "1") if name != "right" else arrived("att_right0")
        if name == "far":
            arrived("att_far0")
        mixed = mixed + project(who)
    mixed_ref[...] = mixed.astype(BF)

    def scans_left():
        @pl.when(z < GROUPS)
        def _():
            y_end(tsum, y_s, y_r, ry, True)
            y_end(t2, gy_s, gy_r, ry2, False)
            for d in ALONG_Z:
                out_state(d, lax.rem(z + d, NZ)).wait_send()
                out_later(d, lax.rem(z + d, NZ)).wait_send()

    sent.append(scans_left)
    finish()


def per_device(queries, keys, values, conv_keys, conv_values, out_weight, cotangent):
    vmem = pltpu.VMEM
    dma = pltpu.SemaphoreType.DMA
    both = 2 * TOK
    scratch = [
        vmem((CONV, 64), F32),
        vmem((CONV, 256), F32),
        vmem((128, 128), F32),
        vmem((32, both), BF),
        vmem((32, 128 + both), BF),
        vmem((HALO + both, 256), BF),
        vmem((512, 2048), BF),
        vmem((NX, TOK, 512), BF),
        vmem((ROWS, both), F32),
        vmem((2, ROWS, both), BF),
        vmem((2, both, ROWS), BF),
        vmem((2, ROWS, both), BF),
        vmem((2, both, ROWS), BF),
        vmem((both, 256), BF),
        vmem((2, 2, TOK, TOK), BF),
        vmem((2, both, 1), F32),
        vmem((ROWS, 256), F32),
        vmem((ROWS, 256), BF),
        vmem((ROWS, 256), BF),
        vmem((4, 128), F32),
        vmem((2, 8, ROWS), F32),
        vmem((NZ, 4, 128), F32),
        vmem((4, 128), F32),
        vmem((NY, 4, 128), F32),
        vmem((NZ, 16, 256), BF),
        vmem((16, 256), F32),
        vmem((NY, 16, 256), F32),
        vmem((16, 256), F32),
        vmem((NZ, 16, 256), BF),
        vmem((ROWS, 256), BF),
        vmem((2, TOK, 256), F32),
        vmem((TOK, 256), F32),
        vmem((both, 256), BF),
        vmem((both, 256), F32),
        vmem((ROWS, 256), F32),
        vmem((ROWS, 256), BF),
        vmem((NZ, 16, 256), BF),
        vmem((16, 256), BF),
        vmem((NY, 16, 256), BF),
        vmem((NZ, 16, 256), BF),
        vmem((ROWS, 256), BF),
        vmem((2, TOK, 256), BF),
        vmem((2, TOK, 256), BF),
        vmem((NX, 2, TOK, 256), BF),
        vmem((NX, 512, 512), BF),
        dma((8,)),
        dma((3,)), dma((3,)),
        dma((4,)), dma((2,)),
        dma((NZ,)), dma((NZ,)), dma((NY,)), dma((NY,)), dma((NZ,)), dma((NZ,)),
        dma((NZ,)), dma((NZ,)), dma((NY,)), dma((NY,)), dma((NZ,)), dma((NZ,)),
        dma((6,)), dma((6,)),
        dma((NZ,)), dma((NZ,)), dma((NY,)), dma((NY,)),
        dma((NX,)), dma((NX,)), dma((NX,)), dma((NX,)), dma((6,)), dma((6,)),
        dma((3,)), dma((3,)),
    ]
    in_hbm = pl.BlockSpec(memory_space=pltpu.HBM)
    in_vmem = pl.BlockSpec(memory_space=pltpu.VMEM)
    out = jax.ShapeDtypeStruct(values.shape, BF)
    return pl.pallas_call(
        body,
        out_shape=(out, out),
        in_specs=[in_hbm] * 7,
        out_specs=(in_vmem, in_vmem),
        scratch_shapes=scratch,
        compiler_params=pltpu.CompilerParams(
            collective_id=0, has_side_effects=True, vmem_limit_bytes=56 << 20
        ),
    )(queries.T, keys.T, values, conv_keys, conv_values, out_weight, cotangent)


def solution(mesh):
    in_specs = (
        P("ctx", "head"),
        P("ctx", "head"),
        P("ctx", "head"),
        P(None, "head"),
        P(None, "head"),
        P("head", None),
        P("ctx", "head"),
    )
    out_specs = (P("ctx", "head"), P("ctx", "head"))
    return jax.shard_map(
        per_device, mesh=mesh, in_specs=in_specs, out_specs=out_specs, check_vma=False
    )
```

```python
import functools

import jax
import jax.numpy as jnp
from jax import lax
from jax.experimental import pallas as pl
from jax.experimental.pallas import tpu as pltpu
from jax.sharding import PartitionSpec as P

FEAT = 16
VDIM = 128
CONV = 3
NY, NZ, NX = 8, 12, 4
TOK = 256
ROWS = 160
GROUPS = ROWS // 16
HALO = 16
ALONG_Z = sorted(range(1, NZ), key=lambda d: -min(d, NZ - d))
ALONG_Y = sorted(range(1, NY), key=lambda d: -min(d, NY - d))
BF = jnp.bfloat16
F32 = jnp.float32


def mm(a, b):
    return jnp.dot(a, b, preferred_element_type=F32)


def mm_t(a, b):
    return lax.dot_general(a, b, (((1,), (1,)), ((), ())), preferred_element_type=F32)


def remote(src, dst, send, recv, ctx, head):
    return pltpu.make_async_remote_copy(
        src_ref=src,
        dst_ref=dst,
        send_sem=send,
        recv_sem=recv,
        device_id=(ctx, head),
        device_id_type=pl.DeviceIdType.MESH,
    )


def build_features(channels, query, store):
    s = channels * FEAT ** (-0.25)
    half = 0.5**0.5
    pair = 2.0 * half if query else half
    store[0:16, :] = s * s * half
    for d in range(1, 8):
        store[16 * d : 16 * d + 16, :] = s * pltpu.roll(s, FEAT - d, 0) * pair
    store[128:136, :] = s[0:8] * s[8:16] * pair
    row = lax.broadcasted_iota(jnp.int32, (8, s.shape[1]), 0)
    store[136:144, :] = jnp.where(row == 0, 1.0, 0.0)
    store[144:160, :] = s


def body(
    q_hbm, k_hbm, v_hbm, ck_hbm, cv_hbm, w_hbm, cot_hbm, out_ref,
    ck, cv, taps, qb, kb, vb, w, cotg, feat, q_pt, q_tp, k_pt, k_tp, vc, wl, dsum,
    state0, a1, n1, own0, nz, nt, ny, r1, tsum, ry, base, qo, pr,
    og, ogs, grad, vin, u1, a2, r2, t2, ry2, qo2, pr2, atts, pri, numi, vgs, lat,
    attg, wcol,
    loc, ex_s, ex_r, halo_s, halo_r, p1_s, p1_r, y_s, y_r, p3_s, p3_r,
    g1_s, g1_r, gy_s, gy_r, g3_s, g3_r, ag_s, ag_r, nz_s, nz_r, ny_s, ny_r, wc_s, wc_r, wf_s, wf_r, at_s, at_r, misc_s, misc_r,
):
    ctx = lax.axis_index("ctx")
    x = lax.axis_index("head")
    y = lax.div(ctx, 2 * NZ)
    chip = lax.div(ctx, 2)
    z = lax.rem(chip, NZ)
    c = lax.rem(ctx, 2)
    sib = chip * 2 + 1 - c
    chips = NY * NZ
    before = lax.rem(chip + chips - 1, chips)
    after = lax.rem(chip + 1, chips)
    right, left = lax.rem(x + 1, NX), lax.rem(x + NX - 1, NX)
    far = lax.rem(x + 2, NX)

    def at(y_, z_):
        return (y_ * NZ + z_) * 2 + c

    barrier = pltpu.get_barrier_semaphore()

    def greet(ctx_, x_):
        pl.semaphore_signal(
            barrier, inc=1, device_id=(ctx_, x_), device_id_type=pl.DeviceIdType.MESH
        )

    for d in ALONG_Z:
        greet(at(y, lax.rem(z + d, NZ)), x)
    for d in ALONG_Y:
        greet(at(lax.rem(y + d, NY), z), x)
    greet(ctx, far)
    greet(before * 2 + 1, x)
    greet(ctx, right)
    greet(ctx, left)
    greet(sib, x)
    sent, due = [], {}

    def go(copy, name=None):
        copy.start()
        sent.append(copy.wait_send)
        if name is not None:
            due[name] = copy.wait_recv
        return copy

    def arrived(name):
        due.pop(name)()

    def finish():
        for name in list(due):
            arrived(name)
        for wait in sent:
            wait()

    own_lanes = pl.ds(pl.multiple_of(256 * c, 256), 256)
    sib_lanes = pl.ds(pl.multiple_of(256 * (1 - c), 256), 256)
    vg_lanes = pl.ds(pl.multiple_of(512 + 256 * c, 256), 256)
    own_rows = pl.ds(pl.multiple_of(32 * c, 32), 32)
    sib_rows = pl.ds(pl.multiple_of(32 * (1 - c), 32), 32)
    mine = pl.ds(pl.multiple_of(HALO + TOK * c, 16), TOK)
    mine_k = pl.ds(pl.multiple_of(128 + TOK * c, 128), TOK)
    loads = [
        pltpu.make_async_copy(ck_hbm, ck, loc.at[5]),
        pltpu.make_async_copy(cv_hbm.at[:, own_lanes], cv, loc.at[6]),
        pltpu.make_async_copy(k_hbm.at[own_rows, :], kb.at[:, mine_k], loc.at[1]),
        pltpu.make_async_copy(q_hbm.at[own_rows, :], qb.at[:, own_lanes], loc.at[3]),
        pltpu.make_async_copy(v_hbm.at[:, own_lanes], vb.at[mine, :], loc.at[2]),
    ]
    for copy in loads:
        copy.start()
    load_c = pltpu.make_async_copy(cot_hbm, cotg.at[x], loc.at[4])
    load_w = pltpu.make_async_copy(w_hbm, w, loc.at[0])
    load_c.start()
    load_w.start()
    due["c"] = load_c.wait
    due["w"] = load_w.wait

    pl.semaphore_wait(barrier, 4 + (NZ - 1) + (NY - 1) + 2 * c)

    last = pl.ds(TOK - HALO, HALO)
    halos = []
    for cc in range(2):
        halos.append(
            remote(
                k_hbm.at[32 * cc : 32 * cc + 32, TOK - 128 : TOK], kb.at[:, 0:128],
                halo_s.at[cc], halo_r.at[0], after * 2 + cc, x,
            )
        )
        halos.append(
            remote(
                v_hbm.at[last, 256 * cc : 256 * cc + 256], vb.at[0:HALO, :],
                halo_s.at[2 + cc], halo_r.at[1], after * 2 + cc, x,
            )
        )

    @pl.when(c == 1)
    def _():
        for copy in halos:
            copy.start()

    def halos_left():
        @pl.when(c == 1)
        def _():
            for copy in halos:
                copy.wait_send()

    sent.append(halos_left)
    due["halo_k"] = halos[0].wait_recv
    due["halo_v"] = halos[1].wait_recv
    go(remote(k_hbm.at[sib_rows, :], kb.at[:, mine_k], ex_s.at[0], ex_r.at[0], sib, x), "k")
    go(remote(v_hbm.at[:, sib_lanes], vb.at[mine, :], ex_s.at[1], ex_r.at[1], sib, x), "v")
    go(remote(q_hbm.at[sib_rows, :], qb.at[:, own_lanes], ex_s.at[2], ex_r.at[2], sib, x), "q")
    def gather(own, slots, sends, recvs, name):
        go(remote(own(0), slots(x, 0), sends.at[0], recvs.at[0], ctx, right), name + "_left0")
        go(remote(own(1), slots(x, 1), sends.at[1], recvs.at[1], ctx, left), name + "_right1")
        go(remote(own(1), slots(x, 1), sends.at[2], recvs.at[2], ctx, right), name + "_left1")
        go(remote(own(0), slots(x, 0), sends.at[3], recvs.at[3], ctx, left), name + "_right0")

    def pass_on(slots, sends, recvs, name):
        arrived(name + "_left0")
        go(remote(slots(left, 0), slots(left, 0), sends.at[4], recvs.at[4], ctx, right), name + "_far0")
        arrived(name + "_right1")
        go(remote(slots(right, 1), slots(right, 1), sends.at[5], recvs.at[5], ctx, left), name + "_far1")

    cot_half = lambda i: pl.ds(TOK // 2 * i, TOK // 2)
    cot_slot = lambda who, i: cotg.at[who, cot_half(i)]
    gather(lambda i: cot_hbm.at[cot_half(i), :], cot_slot, ag_s, ag_r, "cot")

    for copy in loads:
        copy.wait()
    for name in ("k", "v"):
        arrived(name)

    taps[...] = jnp.zeros(taps.shape, F32)
    taps[0:CONV, 0:64] = ck[...]
    taps[...] = taps[...].T
    tap = taps[own_rows, :]

    def key_features(joined, columns):
        key_conv = tap[:, 0:1] * joined[:, 128:]
        for j in range(1, CONV):
            key_conv = key_conv + tap[:, j : j + 1] * pltpu.roll(joined, j, 1)[:, 128:]
        for j in range(2):
            build_features(key_conv[16 * j : 16 * j + 16], False, feat.at[j, :, columns])
            k_pt[j, :, columns] = feat[j, :, columns].astype(BF)

    key_features(
        jnp.concatenate([jnp.zeros((32, 128), F32), kb[:, 128:].astype(F32)], 1),
        slice(0, 2 * TOK),
    )
    arrived("halo_k")
    arrived("halo_v")

    @pl.when(chip == 0)
    def _():
        kb[:, 0:128] = jnp.zeros((32, 128), BF)
        vb[0:HALO, :] = jnp.zeros((HALO, 256), BF)

    key_features(kb[:, 0:256].astype(F32), slice(0, 128))
    pick = lax.broadcasted_iota(jnp.int32, (8, 2 * TOK), 0)
    token = lax.broadcasted_iota(jnp.int32, (8, 2 * TOK), 1)
    ones = jnp.where((pick == 0) | ((pick == 1) & (token < TOK)), 1.0, 0.0).astype(BF)
    n1[...] = jnp.zeros(n1.shape, F32)
    for j in range(2):
        norms = mm_t(ones, k_pt[j])
        n1[2 * j : 2 * j + 1, :] = norms[0:1, 0:128]
        n1[2 * j + 1 : 2 * j + 2, 0 : ROWS - 128] = norms[0:1, 128:]
        own0[j] = norms
    for d in ALONG_Z:
        to = lax.rem(z + d, NZ)
        go(remote(n1, nz.at[z], nz_s.at[d], nz_r.at[z], at(y, to), x))
    nz[z] = n1[...]

    joined = vb[...].astype(F32)
    value_conv = cv[0:1] * joined[HALO:]
    for j in range(1, CONV):
        value_conv = value_conv + cv[j : j + 1] * pltpu.roll(joined, j, 0)[HALO:]
    vc[...] = value_conv.astype(BF)
    for j in range(2):
        lanes = slice(VDIM * j, VDIM * j + VDIM)
        s0 = mm(k_pt[j, :, 0:TOK], vc[0:TOK, lanes])
        state0[:, lanes] = s0
        a1[:, lanes] = (s0 + mm(k_pt[j, :, TOK:], vc[TOK:, lanes])).astype(BF)

    def group(ref, g):
        return ref.at[pl.ds(pl.multiple_of(16 * g, 16), 16), :]

    def spread(source, landing, sends, recvs):
        for d in ALONG_Z:
            to = lax.rem(z + d, NZ)

            @pl.when(to < GROUPS)
            def _():
                remote(
                    group(source, to), landing.at[z], sends.at[d], recvs.at[z], at(y, to), x
                ).start()

    def spread_end(source, landing, sends, recvs):
        for d in ALONG_Z:
            to = lax.rem(z + d, NZ)

            @pl.when(to < GROUPS)
            def _():
                remote(
                    group(source, to), landing.at[z], sends.at[d], recvs.at[z], at(y, to), x
                ).wait_send()

    def sum_up(source, source_like, landing, recvs, sums, ys, yr, landing_y, forward):
        landing[z] = source
        for d in ALONG_Z:
            frm = lax.rem(z + d, NZ)
            remote(source_like, landing.at[frm], ys.at[0], recvs.at[frm], ctx, x).wait_recv()
        acc = landing[0].astype(F32)
        for j in range(1, NZ):
            acc = acc + landing[j].astype(F32)
        sums[...] = acc.astype(sums.dtype)
        for d in ALONG_Y:
            to = y + d if forward else y - d
            need = to < NY if forward else to >= 0

            @pl.when(need)
            def _():
                remote(sums, landing_y.at[y], ys.at[d], yr.at[y], at(to, z), x).start()

    def hand_out(landing, sums, ys, yr, landing_y, start, outs, forward, send_one, keep_own):
        start[...] = jnp.zeros(start.shape, F32)
        for d in ALONG_Y:
            frm = y - d if forward else y + d
            there = frm >= 0 if forward else frm < NY

            @pl.when(there)
            def _():
                remote(sums, landing_y.at[frm], ys.at[0], yr.at[frm], ctx, x).wait_recv()
                start[...] += landing_y[frm].astype(F32)

        run = start[...]
        order = range(NZ) if forward else range(NZ - 1, -1, -1)
        for j in order:
            outs[j] = run.astype(outs.dtype)
            run = run + landing[j].astype(F32)
        for d in ALONG_Z:
            send_one(d, lax.rem(z + d, NZ)).start()
        keep_own(outs[z])

    def y_end(sums, ys, yr, landing_y, forward):
        for d in ALONG_Y:
            to = y + d if forward else y - d
            need = to < NY if forward else to >= 0

            @pl.when(need)
            def _():
                remote(sums, landing_y.at[y], ys.at[d], yr.at[y], at(to, z), x).wait_send()

    spread(a1, r1, p1_s, p1_r)
    sent.append(lambda: spread_end(a1, r1, p1_s, p1_r))

    for j in range(2):
        k_tp[j] = feat[j].T.astype(BF)
    arrived("q")
    for j in range(2):
        build_features(qb[16 * j : 16 * j + 16, :].astype(F32), True, feat.at[j])
        q_pt[j] = feat[j].astype(BF)
        q_tp[j] = feat[j].T.astype(BF)
    t_at = lax.broadcasted_iota(jnp.int32, (TOK, TOK), 0)
    s_at = lax.broadcasted_iota(jnp.int32, (TOK, TOK), 1)
    for j in range(2):
        for b in range(2):
            rows = slice(TOK * b, TOK * b + TOK)
            scores = jnp.where(t_at >= s_at, mm(q_tp[j, rows], k_pt[j, :, rows]), 0.0)
            wl[j, b] = scores.astype(BF)
            dsum[j, rows] = jnp.sum(scores, 1, keepdims=True)

    pass_on(cot_slot, ag_s, ag_r, "cot")

    for d in ALONG_Z:
        frm = lax.rem(z + d, NZ)
        remote(n1, nz.at[frm], nz_s.at[0], nz_r.at[frm], ctx, x).wait_recv()
    acc = nz[0]
    for j in range(1, NZ):
        acc = acc + nz[j]
    nt[...] = acc
    for d in ALONG_Y:

        @pl.when(y + d < NY)
        def _():
            remote(nt, ny.at[y], ny_s.at[d], ny_r.at[y], at(y + d, z), x).start()

    def norms_left():
        for d in ALONG_Y:

            @pl.when(y + d < NY)
            def _():
                remote(nt, ny.at[y], ny_s.at[d], ny_r.at[y], at(y + d, z), x).wait_send()

    sent.append(norms_left)

    half = pl.ds(pl.multiple_of(256 * c, 256), 256)
    for d in (1, 3, 2):
        to = lax.rem(x + d, NX)
        columns = pl.ds(pl.multiple_of(512 * to, 512), 512)
        go(remote(w_hbm.at[half, columns], wcol.at[x, half], wc_s.at[d], wc_r.at[d], ctx, to))
    load_wc = pltpu.make_async_copy(
        w_hbm.at[:, pl.ds(pl.multiple_of(512 * x, 512), 512)], wcol.at[x], loc.at[7]
    )
    load_wc.start()

    arrived("c")
    arrived("w")

    def out_grad(who, row0):
        columns = pl.ds(pl.multiple_of(512 * who, 512), 512)
        return mm_t(cotg[who], w[pl.ds(row0, 256), columns])

    own_row = pl.multiple_of(256 * c, 256)
    sib_row = pl.multiple_of(256 * (1 - c), 256)
    for name in ("cot_left1", "cot_right0"):
        arrived(name)
    ogs[...] = out_grad(x, sib_row) + out_grad(left, sib_row) + out_grad(right, sib_row)
    og[c] = out_grad(x, own_row) + out_grad(left, own_row) + out_grad(right, own_row)

    @pl.when(z < GROUPS)
    def _():
        sum_up(group(a1, z)[...], group(a1, z), r1, p1_r, tsum, y_s, y_r, ry, True)

    arrived("cot_far0")
    arrived("cot_far1")
    ogs[...] += out_grad(far, sib_row)
    go(remote(ogs, og.at[c], misc_s.at[0], misc_r.at[0], sib, x), "og")
    og[c] += out_grad(far, own_row)

    base_n = jnp.zeros((4, 128), F32)
    for j in range(NZ):
        base_n = base_n + jnp.where(j < z, nz[j], 0.0)
    for j in range(NY):

        @pl.when(j >= y)
        def _():
            ny[j] = jnp.zeros((4, 128), F32)

        @pl.when(j < y)
        def _():
            remote(nt, ny.at[j], ny_s.at[0], ny_r.at[j], ctx, x).wait_recv()

    for j in range(NY):
        base_n = base_n + ny[j]
    arrived("og")
    for b in range(2):
        rows = slice(TOK * b, TOK * b + TOK)
        for j in range(2):
            lanes = slice(VDIM * j, VDIM * j + VDIM)
            norm = jnp.concatenate(
                [base_n[2 * j : 2 * j + 1], base_n[2 * j + 1 : 2 * j + 2, 0 : ROWS - 128]], 1
            )
            if b == 1:
                norm = norm + own0[j, 1:2]
            there = jnp.sum(q_tp[j, rows].astype(F32) * norm, 1, keepdims=True)
            inverse = 1.0 / (dsum[j, rows] + there)
            dsum[j, rows] = inverse
            grad[rows, lanes] = (og[b, :, lanes] * inverse).astype(BF)
    for j in range(2):
        lanes = slice(VDIM * j, VDIM * j + VDIM)
        later = mm(q_pt[j, :, TOK:], grad[TOK:, lanes])
        u1[:, lanes] = later
        a2[:, lanes] = (later + mm(q_pt[j, :, 0:TOK], grad[0:TOK, lanes])).astype(BF)
    spread(a2, r2, g1_s, g1_r)
    sent.append(lambda: spread_end(a2, r2, g1_s, g1_r))

    def out_state(d, to):
        return remote(qo.at[to], group(pr, z), p3_s.at[d], p3_r.at[z], at(y, to), x)

    def keep_state(value):
        group(pr, z)[...] = value

    @pl.when(z < GROUPS)
    def _():
        hand_out(r1, tsum, y_s, y_r, ry, base, qo, True, out_state, keep_state)

    for j in range(2):
        lanes = slice(VDIM * j, VDIM * j + VDIM)
        for b in range(2):
            rows = slice(TOK * b, TOK * b + TOK)
            flipped = jnp.where(s_at >= t_at, mm(k_tp[j, rows], q_pt[j, :, rows]), 0.0)
            vin[rows, lanes] = mm(flipped.astype(BF), grad[rows, lanes])

    for j in range(2):
        lanes = slice(VDIM * j, VDIM * j + VDIM)
        for b in range(2):
            rows = slice(TOK * b, TOK * b + TOK)
            numi[rows, lanes] = mm(wl[j, b], vc[rows, lanes])

    @pl.when(z < GROUPS)
    def _():
        sum_up(group(a2, z)[...], group(a2, z), r2, g1_r, t2, gy_s, gy_r, ry2, False)

    for j in range(GROUPS):

        @pl.when(z != j)
        def _():
            remote(
                qo.at[0], pr.at[16 * j : 16 * j + 16, :], p3_s.at[0], p3_r.at[j], ctx, x
            ).wait_recv()

    pri[0] = pr[...]
    pri[1] = (pr[...].astype(F32) + state0[...]).astype(BF)

    def attend(b):
        rows = pl.ds(pl.multiple_of(TOK * b, TOK), TOK)
        parts = []
        for j in range(2):
            lanes = slice(VDIM * j, VDIM * j + VDIM)
            numerator = numi[rows, lanes] + mm(q_tp[j, rows], pri[b, :, lanes])
            parts.append((numerator * dsum[j, rows]).astype(BF))
        return jnp.concatenate(parts, 1)

    atts[...] = attend(1 - c)
    go(remote(atts, attg.at[x, c], misc_s.at[1], misc_r.at[1], sib, x), "att")
    attg[x, c] = attend(c)
    arrived("att")
    att_slot = lambda who, i: attg.at[who, i]
    gather(lambda i: attg.at[x, i], att_slot, at_s, at_r, "att")

    def out_later(d, to):
        return remote(qo2.at[to], group(pr2, z), g3_s.at[d], g3_r.at[z], at(y, to), x)

    def keep_later(value):
        group(pr2, z)[...] = value

    @pl.when(z < GROUPS)
    def _():
        hand_out(r2, t2, gy_s, gy_r, ry2, base, qo2, False, out_later, keep_later)

    for d in (1, 3, 2):
        frm = lax.rem(x + NX - d, NX)
        remote(
            w_hbm.at[half, 0:512], wcol.at[frm, half], wc_s.at[d], wc_r.at[d], ctx, x
        ).wait_recv()
        go(
            remote(wcol.at[frm, half], wcol.at[frm, half], wf_s.at[d], wf_r.at[d], sib, x),
            "wcol%d" % d,
        )

    load_wc.wait()
    for d in (1, 3, 2):
        arrived("wcol%d" % d)

    def project(frm):
        return mm(attg[frm, 0], wcol[frm, 0:256]) + mm(attg[frm, 1], wcol[frm, 256:512])

    mixed = project(x)
    pass_on(att_slot, at_s, at_r, "att")

    for j in range(GROUPS):

        @pl.when(z != j)
        def _():
            remote(
                qo2.at[0], pr2.at[16 * j : 16 * j + 16, :], g3_s.at[0], g3_r.at[j], ctx, x
            ).wait_recv()

    lat[0] = (pr2[...].astype(F32) + u1[...]).astype(BF)
    lat[1] = pr2[...]

    def value_grad(b):
        rows = pl.ds(pl.multiple_of(TOK * b, TOK), TOK)
        parts = []
        for j in range(2):
            lanes = slice(VDIM * j, VDIM * j + VDIM)
            value = vin[rows, lanes] + mm(k_tp[j, rows], lat[b, :, lanes])
            parts.append(value.astype(BF))
        return jnp.concatenate(parts, 1)

    vgs[...] = value_grad(1 - c)
    go(
        remote(vgs, out_ref.at[:, vg_lanes], misc_s.at[2], misc_r.at[2], sib, x),
        "value_grad",
    )
    out_ref[:, vg_lanes] = value_grad(c)

    for who, name in ((left, "att_left1"), (right, "att_right0")):
        arrived(name)
        mixed = mixed + project(who)
    for name in ("att_far0", "att_far1"):
        arrived(name)
    mixed = mixed + project(far)
    out_ref[:, 0:512] = mixed.astype(BF)

    def scans_left():
        @pl.when(z < GROUPS)
        def _():
            y_end(tsum, y_s, y_r, ry, True)
            y_end(t2, gy_s, gy_r, ry2, False)
            for d in ALONG_Z:
                out_state(d, lax.rem(z + d, NZ)).wait_send()
                out_later(d, lax.rem(z + d, NZ)).wait_send()

    sent.append(scans_left)
    finish()


def per_device(queries, keys, values, conv_keys, conv_values, out_weight, cotangent):
    vmem = pltpu.VMEM
    dma = pltpu.SemaphoreType.DMA
    both = 2 * TOK
    scratch = [
        vmem((CONV, 64), F32),
        vmem((CONV, 256), F32),
        vmem((128, 128), F32),
        vmem((32, both), BF),
        vmem((32, 128 + both), BF),
        vmem((HALO + both, 256), BF),
        vmem((512, 2048), BF),
        vmem((NX, TOK, 512), BF),
        vmem((2, ROWS, both), F32),
        vmem((2, ROWS, both), BF),
        vmem((2, both, ROWS), BF),
        vmem((2, ROWS, both), BF),
        vmem((2, both, ROWS), BF),
        vmem((both, 256), BF),
        vmem((2, 2, TOK, TOK), BF),
        vmem((2, both, 1), F32),
        vmem((ROWS, 256), F32),
        vmem((ROWS, 256), BF),
        vmem((4, 128), F32),
        vmem((2, 8, ROWS), F32),
        vmem((NZ, 4, 128), F32),
        vmem((4, 128), F32),
        vmem((NY, 4, 128), F32),
        vmem((NZ, 16, 256), BF),
        vmem((16, 256), BF),
        vmem((NY, 16, 256), BF),
        vmem((16, 256), F32),
        vmem((NZ, 16, 256), BF),
        vmem((ROWS, 256), BF),
        vmem((2, TOK, 256), F32),
        vmem((TOK, 256), F32),
        vmem((both, 256), BF),
        vmem((both, 256), F32),
        vmem((ROWS, 256), F32),
        vmem((ROWS, 256), BF),
        vmem((NZ, 16, 256), BF),
        vmem((16, 256), BF),
        vmem((NY, 16, 256), BF),
        vmem((NZ, 16, 256), BF),
        vmem((ROWS, 256), BF),
        vmem((TOK, 256), BF),
        vmem((2, ROWS, 256), BF),
        vmem((both, 256), F32),
        vmem((TOK, 256), BF),
        vmem((2, ROWS, 256), BF),
        vmem((NX, 2, TOK, 256), BF),
        vmem((NX, 512, 512), BF),
        dma((8,)),
        dma((3,)), dma((3,)),
        dma((4,)), dma((2,)),
        dma((NZ,)), dma((NZ,)), dma((NY,)), dma((NY,)), dma((NZ,)), dma((NZ,)),
        dma((NZ,)), dma((NZ,)), dma((NY,)), dma((NY,)), dma((NZ,)), dma((NZ,)),
        dma((6,)), dma((6,)),
        dma((NZ,)), dma((NZ,)), dma((NY,)), dma((NY,)),
        dma((NX,)), dma((NX,)), dma((NX,)), dma((NX,)), dma((6,)), dma((6,)),
        dma((3,)), dma((3,)),
    ]
    in_hbm = pl.BlockSpec(memory_space=pltpu.HBM)
    in_vmem = pl.BlockSpec(memory_space=pltpu.VMEM)
    out = jax.ShapeDtypeStruct((TOK, 1024), BF)
    both_out = pl.pallas_call(
        body,
        out_shape=out,
        in_specs=[in_hbm] * 7,
        out_specs=in_vmem,
        scratch_shapes=scratch,
        compiler_params=pltpu.CompilerParams(
            collective_id=0, has_side_effects=True, vmem_limit_bytes=56 << 20
        ),
    )(queries.T, keys.T, values, conv_keys, conv_values, out_weight, cotangent)
    return both_out[:, 0:512], both_out[:, 512:1024]


def solution(mesh):
    in_specs = (
        P("ctx", "head"),
        P("ctx", "head"),
        P("ctx", "head"),
        P(None, "head"),
        P(None, "head"),
        P("head", None),
        P("ctx", "head"),
    )
    out_specs = (P("ctx", "head"), P("ctx", "head"))
    return jax.shard_map(
        per_device, mesh=mesh, in_specs=in_specs, out_specs=out_specs, check_vma=False
    )
```

```python
import functools

import jax
import jax.numpy as jnp
from jax import lax
from jax.experimental import pallas as pl
from jax.experimental.pallas import tpu as pltpu
from jax.sharding import PartitionSpec as P

FEAT = 16
VDIM = 128
CONV = 3
NY, NZ, NX = 8, 12, 4
TOK = 256
ROWS = 160
GROUPS = ROWS // 16
HALO = 16
ALONG_Z = sorted(range(1, NZ), key=lambda d: -min(d, NZ - d))
ALONG_Y = sorted(range(1, NY), key=lambda d: -min(d, NY - d))
BF = jnp.bfloat16
F32 = jnp.float32


def mm(a, b):
    return jnp.dot(a, b, preferred_element_type=F32)


def mm_t(a, b):
    return lax.dot_general(a, b, (((1,), (1,)), ((), ())), preferred_element_type=F32)


def remote(src, dst, send, recv, ctx, head):
    return pltpu.make_async_remote_copy(
        src_ref=src,
        dst_ref=dst,
        send_sem=send,
        recv_sem=recv,
        device_id=(ctx, head),
        device_id_type=pl.DeviceIdType.MESH,
    )


def build_features(channels, query, store):
    s = channels * FEAT ** (-0.25)
    half = 0.5**0.5
    pair = 2.0 * half if query else half
    store[0:16, :] = s * s * half
    for d in range(1, 8):
        store[16 * d : 16 * d + 16, :] = s * pltpu.roll(s, FEAT - d, 0) * pair
    store[128:136, :] = s[0:8] * s[8:16] * pair
    row = lax.broadcasted_iota(jnp.int32, (8, s.shape[1]), 0)
    store[136:144, :] = jnp.where(row == 0, 1.0, 0.0)
    store[144:160, :] = s


def body(
    q_hbm, k_hbm, v_hbm, ck_hbm, cv_hbm, w_hbm, cot_hbm, out_ref,
    ck, cv, taps, qb, kb, vb, w, cotg, feat, q_pt, q_tp, k_pt, k_tp, vc, wl, dsum,
    state0, a1, n1, own0, nz, nt, ny, r1, tsum, ry, base, qo, pr,
    og, ogs, grad, vin, u1, a2, r2, t2, ry2, qo2, pr2, atts, pri, numi, vgs, lat,
    attg, wcol,
    loc, ex_s, ex_r, halo_s, halo_r, p1_s, p1_r, y_s, y_r, p3_s, p3_r,
    g1_s, g1_r, gy_s, gy_r, g3_s, g3_r, ag_s, ag_r, nz_s, nz_r, ny_s, ny_r, wc_s, wc_r, wf_s, wf_r, at_s, at_r, misc_s, misc_r,
):
    ctx = lax.axis_index("ctx")
    x = lax.axis_index("head")
    y = lax.div(ctx, 2 * NZ)
    chip = lax.div(ctx, 2)
    z = lax.rem(chip, NZ)
    c = lax.rem(ctx, 2)
    sib = chip * 2 + 1 - c
    chips = NY * NZ
    before = lax.rem(chip + chips - 1, chips)
    after = lax.rem(chip + 1, chips)
    right, left = lax.rem(x + 1, NX), lax.rem(x + NX - 1, NX)
    far = lax.rem(x + 2, NX)

    def at(y_, z_):
        return (y_ * NZ + z_) * 2 + c

    barrier = pltpu.get_barrier_semaphore()

    def greet(ctx_, x_):
        pl.semaphore_signal(
            barrier, inc=1, device_id=(ctx_, x_), device_id_type=pl.DeviceIdType.MESH
        )

    for d in ALONG_Z:
        greet(at(y, lax.rem(z + d, NZ)), x)
    for d in ALONG_Y:
        greet(at(lax.rem(y + d, NY), z), x)
    greet(ctx, far)
    greet(before * 2 + 1, x)
    greet(ctx, right)
    greet(ctx, left)
    greet(sib, x)
    sent, due = [], {}

    def go(copy, name=None):
        copy.start()
        sent.append(copy.wait_send)
        if name is not None:
            due[name] = copy.wait_recv
        return copy

    def arrived(name):
        due.pop(name)()

    def finish():
        for name in list(due):
            arrived(name)
        for wait in sent:
            wait()

    own_lanes = pl.ds(pl.multiple_of(256 * c, 256), 256)
    sib_lanes = pl.ds(pl.multiple_of(256 * (1 - c), 256), 256)
    vg_lanes = pl.ds(pl.multiple_of(512 + 256 * c, 256), 256)
    own_rows = pl.ds(pl.multiple_of(32 * c, 32), 32)
    sib_rows = pl.ds(pl.multiple_of(32 * (1 - c), 32), 32)
    mine = pl.ds(pl.multiple_of(HALO + TOK * c, 16), TOK)
    mine_k = pl.ds(pl.multiple_of(128 + TOK * c, 128), TOK)
    loads = [
        pltpu.make_async_copy(ck_hbm, ck, loc.at[5]),
        pltpu.make_async_copy(cv_hbm.at[:, own_lanes], cv, loc.at[6]),
        pltpu.make_async_copy(k_hbm.at[own_rows, :], kb.at[:, mine_k], loc.at[1]),
        pltpu.make_async_copy(q_hbm.at[own_rows, :], qb.at[:, own_lanes], loc.at[3]),
        pltpu.make_async_copy(v_hbm.at[:, own_lanes], vb.at[mine, :], loc.at[2]),
    ]
    for copy in loads:
        copy.start()
    load_c = pltpu.make_async_copy(cot_hbm, cotg.at[x], loc.at[4])
    load_w = pltpu.make_async_copy(w_hbm, w, loc.at[0])
    load_c.start()
    load_w.start()
    due["c"] = load_c.wait
    due["w"] = load_w.wait

    pl.semaphore_wait(barrier, 4 + (NZ - 1) + (NY - 1) + 2 * c)

    last = pl.ds(TOK - HALO, HALO)
    halos = []
    for cc in range(2):
        halos.append(
            remote(
                k_hbm.at[32 * cc : 32 * cc + 32, TOK - 128 : TOK], kb.at[:, 0:128],
                halo_s.at[cc], halo_r.at[0], after * 2 + cc, x,
            )
        )
        halos.append(
            remote(
                v_hbm.at[last, 256 * cc : 256 * cc + 256], vb.at[0:HALO, :],
                halo_s.at[2 + cc], halo_r.at[1], after * 2 + cc, x,
            )
        )

    @pl.when(c == 1)
    def _():
        for copy in halos:
            copy.start()

    def halos_left():
        @pl.when(c == 1)
        def _():
            for copy in halos:
                copy.wait_send()

    sent.append(halos_left)
    due["halo_k"] = halos[0].wait_recv
    due["halo_v"] = halos[1].wait_recv
    go(remote(k_hbm.at[sib_rows, :], kb.at[:, mine_k], ex_s.at[0], ex_r.at[0], sib, x), "k")
    go(remote(v_hbm.at[:, sib_lanes], vb.at[mine, :], ex_s.at[1], ex_r.at[1], sib, x), "v")
    go(remote(q_hbm.at[sib_rows, :], qb.at[:, own_lanes], ex_s.at[2], ex_r.at[2], sib, x), "q")
    def gather(own, slots, sends, recvs, name):
        go(remote(own(0), slots(x, 0), sends.at[0], recvs.at[0], ctx, right), name + "_left0")
        go(remote(own(1), slots(x, 1), sends.at[1], recvs.at[1], ctx, left), name + "_right1")
        go(remote(own(1), slots(x, 1), sends.at[2], recvs.at[2], ctx, right), name + "_left1")
        go(remote(own(0), slots(x, 0), sends.at[3], recvs.at[3], ctx, left), name + "_right0")

    def pass_on(slots, sends, recvs, name):
        arrived(name + "_left0")
        go(remote(slots(left, 0), slots(left, 0), sends.at[4], recvs.at[4], ctx, right), name + "_far0")
        arrived(name + "_right1")
        go(remote(slots(right, 1), slots(right, 1), sends.at[5], recvs.at[5], ctx, left), name + "_far1")

    cot_half = lambda i: pl.ds(TOK // 2 * i, TOK // 2)
    cot_slot = lambda who, i: cotg.at[who, cot_half(i)]
    gather(lambda i: cot_hbm.at[cot_half(i), :], cot_slot, ag_s, ag_r, "cot")

    for copy in loads:
        copy.wait()
    for name in ("k", "v"):
        arrived(name)

    taps[...] = jnp.zeros(taps.shape, F32)
    taps[0:CONV, 0:64] = ck[...]
    taps[...] = taps[...].T
    tap = taps[own_rows, :]

    def key_features(joined, columns):
        key_conv = tap[:, 0:1] * joined[:, 128:]
        for j in range(1, CONV):
            key_conv = key_conv + tap[:, j : j + 1] * pltpu.roll(joined, j, 1)[:, 128:]
        for j in range(2):
            build_features(key_conv[16 * j : 16 * j + 16], False, feat.at[j, :, columns])
            k_pt[j, :, columns] = feat[j, :, columns].astype(BF)

    key_features(
        jnp.concatenate([jnp.zeros((32, 128), F32), kb[:, 128:].astype(F32)], 1),
        slice(0, 2 * TOK),
    )

    def value_conv(joined):
        out = cv[0:1] * joined[HALO:]
        for j in range(1, CONV):
            out = out + cv[j : j + 1] * pltpu.roll(joined, j, 0)[HALO:]
        return out.astype(BF)

    vc[...] = value_conv(
        jnp.concatenate([jnp.zeros((HALO, 256), F32), vb[HALO:, :].astype(F32)], 0)
    )
    arrived("halo_k")
    arrived("halo_v")

    @pl.when(chip == 0)
    def _():
        kb[:, 0:128] = jnp.zeros((32, 128), BF)
        vb[0:HALO, :] = jnp.zeros((HALO, 256), BF)

    key_features(kb[:, 0:256].astype(F32), slice(0, 128))
    pick = lax.broadcasted_iota(jnp.int32, (8, 2 * TOK), 0)
    token = lax.broadcasted_iota(jnp.int32, (8, 2 * TOK), 1)
    ones = jnp.where((pick == 0) | ((pick == 1) & (token < TOK)), 1.0, 0.0).astype(BF)
    n1[...] = jnp.zeros(n1.shape, F32)
    for j in range(2):
        norms = mm_t(ones, k_pt[j])
        n1[2 * j : 2 * j + 1, :] = norms[0:1, 0:128]
        n1[2 * j + 1 : 2 * j + 2, 0 : ROWS - 128] = norms[0:1, 128:]
        own0[j] = norms
    for d in ALONG_Z:
        to = lax.rem(z + d, NZ)
        go(remote(n1, nz.at[z], nz_s.at[d], nz_r.at[z], at(y, to), x))
    nz[z] = n1[...]

    vc[0:HALO, :] = value_conv(vb[0 : 2 * HALO, :].astype(F32))
    for j in range(2):
        lanes = slice(VDIM * j, VDIM * j + VDIM)
        s0 = mm(k_pt[j, :, 0:TOK], vc[0:TOK, lanes])
        state0[:, lanes] = s0
        a1[:, lanes] = (s0 + mm(k_pt[j, :, TOK:], vc[TOK:, lanes])).astype(BF)

    def group(ref, g):
        return ref.at[pl.ds(pl.multiple_of(16 * g, 16), 16), :]

    def spread(source, landing, sends, recvs):
        for d in ALONG_Z:
            to = lax.rem(z + d, NZ)

            @pl.when(to < GROUPS)
            def _():
                remote(
                    group(source, to), landing.at[z], sends.at[d], recvs.at[z], at(y, to), x
                ).start()

    def spread_end(source, landing, sends, recvs):
        for d in ALONG_Z:
            to = lax.rem(z + d, NZ)

            @pl.when(to < GROUPS)
            def _():
                remote(
                    group(source, to), landing.at[z], sends.at[d], recvs.at[z], at(y, to), x
                ).wait_send()

    def sum_up(source, source_like, landing, recvs, sums, ys, yr, landing_y, forward):
        landing[z] = source
        for d in ALONG_Z:
            frm = lax.rem(z + d, NZ)
            remote(source_like, landing.at[frm], ys.at[0], recvs.at[frm], ctx, x).wait_recv()
        acc = landing[0].astype(F32)
        for j in range(1, NZ):
            acc = acc + landing[j].astype(F32)
        sums[...] = acc.astype(sums.dtype)
        for d in ALONG_Y:
            to = y + d if forward else y - d
            need = to < NY if forward else to >= 0

            @pl.when(need)
            def _():
                remote(sums, landing_y.at[y], ys.at[d], yr.at[y], at(to, z), x).start()

    def hand_out(landing, sums, ys, yr, landing_y, start, outs, forward, send_one, keep_own):
        start[...] = jnp.zeros(start.shape, F32)
        for d in ALONG_Y:
            frm = y - d if forward else y + d
            there = frm >= 0 if forward else frm < NY

            @pl.when(there)
            def _():
                remote(sums, landing_y.at[frm], ys.at[0], yr.at[frm], ctx, x).wait_recv()
                start[...] += landing_y[frm].astype(F32)

        run = start[...]
        order = range(NZ) if forward else range(NZ - 1, -1, -1)
        for j in order:
            outs[j] = run.astype(outs.dtype)
            run = run + landing[j].astype(F32)
        for d in ALONG_Z:
            send_one(d, lax.rem(z + d, NZ)).start()
        keep_own(outs[z])

    def y_end(sums, ys, yr, landing_y, forward):
        for d in ALONG_Y:
            to = y + d if forward else y - d
            need = to < NY if forward else to >= 0

            @pl.when(need)
            def _():
                remote(sums, landing_y.at[y], ys.at[d], yr.at[y], at(to, z), x).wait_send()

    spread(a1, r1, p1_s, p1_r)
    sent.append(lambda: spread_end(a1, r1, p1_s, p1_r))

    for j in range(2):
        k_tp[j] = feat[j].T.astype(BF)
    arrived("q")
    for j in range(2):
        build_features(qb[16 * j : 16 * j + 16, :].astype(F32), True, feat.at[j])
        q_pt[j] = feat[j].astype(BF)
        q_tp[j] = feat[j].T.astype(BF)
    t_at = lax.broadcasted_iota(jnp.int32, (TOK, TOK), 0)
    s_at = lax.broadcasted_iota(jnp.int32, (TOK, TOK), 1)
    for j in range(2):
        for b in range(2):
            rows = slice(TOK * b, TOK * b + TOK)
            scores = jnp.where(t_at >= s_at, mm(q_tp[j, rows], k_pt[j, :, rows]), 0.0)
            wl[j, b] = scores.astype(BF)
            dsum[j, rows] = jnp.sum(scores, 1, keepdims=True)

    pass_on(cot_slot, ag_s, ag_r, "cot")

    for d in ALONG_Z:
        frm = lax.rem(z + d, NZ)
        remote(n1, nz.at[frm], nz_s.at[0], nz_r.at[frm], ctx, x).wait_recv()
    acc = nz[0]
    for j in range(1, NZ):
        acc = acc + nz[j]
    nt[...] = acc
    for d in ALONG_Y:

        @pl.when(y + d < NY)
        def _():
            remote(nt, ny.at[y], ny_s.at[d], ny_r.at[y], at(y + d, z), x).start()

    def norms_left():
        for d in ALONG_Y:

            @pl.when(y + d < NY)
            def _():
                remote(nt, ny.at[y], ny_s.at[d], ny_r.at[y], at(y + d, z), x).wait_send()

    sent.append(norms_left)

    half = pl.ds(pl.multiple_of(256 * c, 256), 256)
    for d in (1, 3, 2):
        to = lax.rem(x + d, NX)
        columns = pl.ds(pl.multiple_of(512 * to, 512), 512)
        go(remote(w_hbm.at[half, columns], wcol.at[x, half], wc_s.at[d], wc_r.at[d], ctx, to))
    load_wc = pltpu.make_async_copy(
        w_hbm.at[:, pl.ds(pl.multiple_of(512 * x, 512), 512)], wcol.at[x], loc.at[7]
    )
    load_wc.start()

    arrived("c")
    arrived("w")

    def out_grad(who, row0):
        columns = pl.ds(pl.multiple_of(512 * who, 512), 512)
        return mm_t(cotg[who], w[pl.ds(row0, 256), columns])

    own_row = pl.multiple_of(256 * c, 256)
    sib_row = pl.multiple_of(256 * (1 - c), 256)
    for name in ("cot_left1", "cot_right0"):
        arrived(name)
    ogs[...] = out_grad(x, sib_row) + out_grad(left, sib_row) + out_grad(right, sib_row)
    og[c] = out_grad(x, own_row) + out_grad(left, own_row) + out_grad(right, own_row)

    @pl.when(z < GROUPS)
    def _():
        sum_up(group(a1, z)[...], group(a1, z), r1, p1_r, tsum, y_s, y_r, ry, True)

    arrived("cot_far0")
    arrived("cot_far1")
    ogs[...] += out_grad(far, sib_row)
    go(remote(ogs, og.at[c], misc_s.at[0], misc_r.at[0], sib, x), "og")
    og[c] += out_grad(far, own_row)

    base_n = jnp.zeros((4, 128), F32)
    for j in range(NZ):
        base_n = base_n + jnp.where(j < z, nz[j], 0.0)
    for j in range(NY):

        @pl.when(j >= y)
        def _():
            ny[j] = jnp.zeros((4, 128), F32)

        @pl.when(j < y)
        def _():
            remote(nt, ny.at[j], ny_s.at[0], ny_r.at[j], ctx, x).wait_recv()

    for j in range(NY):
        base_n = base_n + ny[j]
    arrived("og")
    for b in range(2):
        rows = slice(TOK * b, TOK * b + TOK)
        for j in range(2):
            lanes = slice(VDIM * j, VDIM * j + VDIM)
            norm = jnp.concatenate(
                [base_n[2 * j : 2 * j + 1], base_n[2 * j + 1 : 2 * j + 2, 0 : ROWS - 128]], 1
            )
            if b == 1:
                norm = norm + own0[j, 1:2]
            there = jnp.sum(q_tp[j, rows].astype(F32) * norm, 1, keepdims=True)
            inverse = 1.0 / (dsum[j, rows] + there)
            dsum[j, rows] = inverse
            grad[rows, lanes] = (og[b, :, lanes] * inverse).astype(BF)
    for j in range(2):
        lanes = slice(VDIM * j, VDIM * j + VDIM)
        later = mm(q_pt[j, :, TOK:], grad[TOK:, lanes])
        u1[:, lanes] = later
        a2[:, lanes] = (later + mm(q_pt[j, :, 0:TOK], grad[0:TOK, lanes])).astype(BF)
    spread(a2, r2, g1_s, g1_r)
    sent.append(lambda: spread_end(a2, r2, g1_s, g1_r))

    def out_state(d, to):
        return remote(qo.at[to], group(pr, z), p3_s.at[d], p3_r.at[z], at(y, to), x)

    def keep_state(value):
        group(pr, z)[...] = value

    @pl.when(z < GROUPS)
    def _():
        hand_out(r1, tsum, y_s, y_r, ry, base, qo, True, out_state, keep_state)

    for j in range(2):
        lanes = slice(VDIM * j, VDIM * j + VDIM)
        for b in range(2):
            rows = slice(TOK * b, TOK * b + TOK)
            numi[rows, lanes] = mm(wl[j, b], vc[rows, lanes])

    @pl.when(z < GROUPS)
    def _():
        sum_up(group(a2, z)[...], group(a2, z), r2, g1_r, t2, gy_s, gy_r, ry2, False)

    for j in range(GROUPS):

        @pl.when(z != j)
        def _():
            remote(
                qo.at[0], pr.at[16 * j : 16 * j + 16, :], p3_s.at[0], p3_r.at[j], ctx, x
            ).wait_recv()

    pri[0] = pr[...]
    pri[1] = (pr[...].astype(F32) + state0[...]).astype(BF)

    def attend(b):
        rows = pl.ds(pl.multiple_of(TOK * b, TOK), TOK)
        parts = []
        for j in range(2):
            lanes = slice(VDIM * j, VDIM * j + VDIM)
            numerator = numi[rows, lanes] + mm(q_tp[j, rows], pri[b, :, lanes])
            parts.append((numerator * dsum[j, rows]).astype(BF))
        return jnp.concatenate(parts, 1)

    att_slot = lambda who, i: attg.at[who, i]

    def send_half(i):
        mine_half = attg.at[x, i]
        go(remote(mine_half, mine_half, at_s.at[2 * i], at_r.at[2 * i], ctx, right))
        go(remote(mine_half, mine_half, at_s.at[3 - 2 * i], at_r.at[3 - 2 * i], ctx, left))

    for i in range(2):
        due["att_left%d" % i] = remote(
            attg.at[left, i], attg.at[left, i], at_s.at[2 * i], at_r.at[2 * i], ctx, right
        ).wait_recv
        due["att_right%d" % i] = remote(
            attg.at[right, i], attg.at[right, i], at_s.at[3 - 2 * i], at_r.at[3 - 2 * i], ctx, left
        ).wait_recv
    attg[x, c] = attend(c)
    send_half(c)
    atts[...] = attend(1 - c)
    go(remote(atts, attg.at[x, c], misc_s.at[1], misc_r.at[1], sib, x), "att")
    arrived("att")
    send_half(1 - c)

    def out_later(d, to):
        return remote(qo2.at[to], group(pr2, z), g3_s.at[d], g3_r.at[z], at(y, to), x)

    def keep_later(value):
        group(pr2, z)[...] = value

    @pl.when(z < GROUPS)
    def _():
        hand_out(r2, t2, gy_s, gy_r, ry2, base, qo2, False, out_later, keep_later)

    pass_on(att_slot, at_s, at_r, "att")
    for j in range(2):
        lanes = slice(VDIM * j, VDIM * j + VDIM)
        for b in range(2):
            rows = slice(TOK * b, TOK * b + TOK)
            flipped = jnp.where(s_at >= t_at, mm(k_tp[j, rows], q_pt[j, :, rows]), 0.0)
            vin[rows, lanes] = mm(flipped.astype(BF), grad[rows, lanes])

    for d in (1, 3, 2):
        frm = lax.rem(x + NX - d, NX)
        remote(
            w_hbm.at[half, 0:512], wcol.at[frm, half], wc_s.at[d], wc_r.at[d], ctx, x
        ).wait_recv()
        go(
            remote(wcol.at[frm, half], wcol.at[frm, half], wf_s.at[d], wf_r.at[d], sib, x),
            "wcol%d" % d,
        )

    load_wc.wait()
    for d in (1, 3, 2):
        arrived("wcol%d" % d)

    def project(frm):
        return mm(attg[frm, 0], wcol[frm, 0:256]) + mm(attg[frm, 1], wcol[frm, 256:512])

    mixed = project(x)

    for j in range(GROUPS):

        @pl.when(z != j)
        def _():
            remote(
                qo2.at[0], pr2.at[16 * j : 16 * j + 16, :], g3_s.at[0], g3_r.at[j], ctx, x
            ).wait_recv()

    lat[0] = (pr2[...].astype(F32) + u1[...]).astype(BF)
    lat[1] = pr2[...]

    def value_grad(b):
        rows = pl.ds(pl.multiple_of(TOK * b, TOK), TOK)
        parts = []
        for j in range(2):
            lanes = slice(VDIM * j, VDIM * j + VDIM)
            value = vin[rows, lanes] + mm(k_tp[j, rows], lat[b, :, lanes])
            parts.append(value.astype(BF))
        return jnp.concatenate(parts, 1)

    vgs[...] = value_grad(1 - c)
    go(
        remote(vgs, out_ref.at[:, vg_lanes], misc_s.at[2], misc_r.at[2], sib, x),
        "value_grad",
    )
    out_ref[:, vg_lanes] = value_grad(c)

    for who, name in ((left, "att_left1"), (right, "att_right0")):
        arrived(name)
        mixed = mixed + project(who)
    for name in ("att_far0", "att_far1"):
        arrived(name)
    mixed = mixed + project(far)
    out_ref[:, 0:512] = mixed.astype(BF)

    def scans_left():
        @pl.when(z < GROUPS)
        def _():
            y_end(tsum, y_s, y_r, ry, True)
            y_end(t2, gy_s, gy_r, ry2, False)
            for d in ALONG_Z:
                out_state(d, lax.rem(z + d, NZ)).wait_send()
                out_later(d, lax.rem(z + d, NZ)).wait_send()

    sent.append(scans_left)
    finish()


def per_device(queries, keys, values, conv_keys, conv_values, out_weight, cotangent):
    vmem = pltpu.VMEM
    dma = pltpu.SemaphoreType.DMA
    both = 2 * TOK
    scratch = [
        vmem((CONV, 64), F32),
        vmem((CONV, 256), F32),
        vmem((128, 128), F32),
        vmem((32, both), BF),
        vmem((32, 128 + both), BF),
        vmem((HALO + both, 256), BF),
        vmem((512, 2048), BF),
        vmem((NX, TOK, 512), BF),
        vmem((2, ROWS, both), F32),
        vmem((2, ROWS, both), BF),
        vmem((2, both, ROWS), BF),
        vmem((2, ROWS, both), BF),
        vmem((2, both, ROWS), BF),
        vmem((both, 256), BF),
        vmem((2, 2, TOK, TOK), BF),
        vmem((2, both, 1), F32),
        vmem((ROWS, 256), F32),
        vmem((ROWS, 256), BF),
        vmem((4, 128), F32),
        vmem((2, 8, ROWS), F32),
        vmem((NZ, 4, 128), F32),
        vmem((4, 128), F32),
        vmem((NY, 4, 128), F32),
        vmem((NZ, 16, 256), BF),
        vmem((16, 256), BF),
        vmem((NY, 16, 256), BF),
        vmem((16, 256), F32),
        vmem((NZ, 16, 256), BF),
        vmem((ROWS, 256), BF),
        vmem((2, TOK, 256), F32),
        vmem((TOK, 256), F32),
        vmem((both, 256), BF),
        vmem((both, 256), F32),
        vmem((ROWS, 256), F32),
        vmem((ROWS, 256), BF),
        vmem((NZ, 16, 256), BF),
        vmem((16, 256), BF),
        vmem((NY, 16, 256), BF),
        vmem((NZ, 16, 256), BF),
        vmem((ROWS, 256), BF),
        vmem((TOK, 256), BF),
        vmem((2, ROWS, 256), BF),
        vmem((both, 256), F32),
        vmem((TOK, 256), BF),
        vmem((2, ROWS, 256), BF),
        vmem((NX, 2, TOK, 256), BF),
        vmem((NX, 512, 512), BF),
        dma((8,)),
        dma((3,)), dma((3,)),
        dma((4,)), dma((2,)),
        dma((NZ,)), dma((NZ,)), dma((NY,)), dma((NY,)), dma((NZ,)), dma((NZ,)),
        dma((NZ,)), dma((NZ,)), dma((NY,)), dma((NY,)), dma((NZ,)), dma((NZ,)),
        dma((6,)), dma((6,)),
        dma((NZ,)), dma((NZ,)), dma((NY,)), dma((NY,)),
        dma((NX,)), dma((NX,)), dma((NX,)), dma((NX,)), dma((6,)), dma((6,)),
        dma((3,)), dma((3,)),
    ]
    in_hbm = pl.BlockSpec(memory_space=pltpu.HBM)
    in_vmem = pl.BlockSpec(memory_space=pltpu.VMEM)
    out = jax.ShapeDtypeStruct((TOK, 1024), BF)
    both_out = pl.pallas_call(
        body,
        out_shape=out,
        in_specs=[in_hbm] * 7,
        out_specs=in_vmem,
        scratch_shapes=scratch,
        compiler_params=pltpu.CompilerParams(
            collective_id=0, has_side_effects=True, vmem_limit_bytes=56 << 20
        ),
    )(queries.T, keys.T, values, conv_keys, conv_values, out_weight, cotangent)
    return both_out[:, 0:512], both_out[:, 512:1024]


def solution(mesh):
    in_specs = (
        P("ctx", "head"),
        P("ctx", "head"),
        P("ctx", "head"),
        P(None, "head"),
        P(None, "head"),
        P("head", None),
        P("ctx", "head"),
    )
    out_specs = (P("ctx", "head"), P("ctx", "head"))
    return jax.shard_map(
        per_device, mesh=mesh, in_specs=in_specs, out_specs=out_specs, check_vma=False
    )
```
